512 devices in a mesh: pole: 8 (over z_hi, y), space: 64 (over z_lo, x, core).
Axes of the slice: x: 4, y: 4, z: 16 (z_hi: 2, z_lo: 8; z = z_hi * 8 + z_lo), core: 2. Of those that a mesh axis runs over, the one named last changes fastest.
Arguments:
- conductivity: float32 [128, 64, 128], P('space'), may hold values from 0.1 to 10
- misfit: float32 [128, 64, 128], P('space'), may hold values from -6 to 6
- forward_states: float32 [16, 128, 64, 128], P('pole', 'space'), may hold values from -6 to 6
- pole_shifts: float32 [16], replicated, may hold values from 0.01 to 10
- pole_weights: float32 [16], replicated, may hold values from 0.05 to 1
- pole_order: int32 [16], P('pole'), may hold values from 0 to 15, each once
Outputs:
- adjoint_states: float32 [16, 128, 64, 128], P('pole', 'space')
- gradient: float32 [128, 64, 128], P('space', 'pole')
The draws below stay inside these ranges and needn't reach their ends.
Inputs may be any that keep to these rules, and one draw needn't show every extreme that they name: `pole_order`: every pole stands in exactly one slot.
All inputs are finite; a program needn't handle non-finite values.
Results may differ from the reference program's by a relative error of at most 0.0001.
Values sent between devices are 32-bit elements; how exact they have to be, the bound alone decides.
A program may use at most 128 MiB of HBM per device.

```python
import math
import jax
import jax.numpy as jnp
from jax import lax

NY = 64
NZ = 128
ITERS = 2
POLES = 16
NX = 128


def block_levels(key, shape, cuts, low, largest):
    factor_of = 1.0
    for dim, blocks in cuts:
        steps = jax.random.uniform(jax.random.fold_in(jax.random.fold_in(key, 6), dim), (blocks,), jnp.float32, low / len(cuts), largest / len(cuts))
        factor_of = factor_of * jnp.repeat(jnp.exp(steps), shape[dim] // blocks).reshape((-1,) + (1,) * (len(shape) - 1 - dim))
    return factor_of


def centred(own_key, dims, deviation, bound, shards=(), dtype=jnp.bfloat16):
    array = deviation * jax.random.normal(own_key, dims, jnp.float32)
    if shards:
        array = array * block_levels(own_key, dims, shards, -0.22, 0.18)
    return jnp.clip(array, -bound, bound).astype(dtype)


def setup_inputs(seed: int = 0) -> dict:
    key_of = jax.random.split(jax.random.key(seed), 7)
    conductivity = jnp.clip(jnp.exp(math.log(10.0) - 4.6051702 * jax.random.uniform(key_of[0], (NX, NY, NZ), jnp.float32) ** block_levels(key_of[0], (NX, NY, NZ), ((0, 64),), -0.2, 0.2)), 0.1, 10.0)
    misfit = centred(key_of[1], (NX, NY, NZ), 1.0, 6.0, ((0, 64),), jnp.float32)
    forward_states = centred(key_of[2], (POLES, NX, NY, NZ), 1.0, 6.0, ((0, 8), (1, 64)), jnp.float32)
    pole_shifts = jnp.clip(jnp.exp(jax.random.uniform(key_of[3], (POLES,), jnp.float32, math.log(0.01), math.log(10.0))), 0.01, 10.0)
    pole_weights = jnp.clip(jnp.exp(jax.random.uniform(key_of[4], (POLES,), jnp.float32, math.log(0.05), math.log(1.0))), 0.05, 1.0)
    pole_order = jax.random.permutation(key_of[5], POLES).astype(jnp.int32)
    return dict(conductivity=conductivity, misfit=misfit, forward_states=forward_states, pole_shifts=pole_shifts, pole_weights=pole_weights, pole_order=pole_order)


DAMPING = 0.8


def plus_side(field, which_dim):
    extent = field.shape[which_dim]
    inner_part = lax.slice_in_dim(field, 1, extent, axis=which_dim)
    zero_plane = jnp.zeros_like(lax.slice_in_dim(field, 0, 1, axis=which_dim))
    return jnp.concatenate([inner_part, zero_plane], axis=which_dim)


def minus_side(field, which_dim):
    extent = field.shape[which_dim]
    inner_part = lax.slice_in_dim(field, 0, extent - 1, axis=which_dim)
    zero_plane = jnp.zeros_like(lax.slice_in_dim(field, 0, 1, axis=which_dim))
    return jnp.concatenate([zero_plane, inner_part], axis=which_dim)


def coarse_pick(faces, which_dim, offset):
    extent_x, extent_y, extent_z = faces.shape
    blocks = faces.reshape(extent_x // 2, 2, extent_y // 2, 2, extent_z // 2, 2)
    chosen = lax.index_in_dim(blocks, offset, axis=2 * which_dim + 1, keepdims=True)
    return jnp.sum(chosen, axis=(1, 3, 5))


def operate(field, plus_faces, minus_faces, shift_value):
    result = shift_value * field
    for which_dim in range(3):
        result = result + plus_faces[which_dim] * (field - plus_side(field, which_dim))
        result = result + minus_faces[which_dim] * (field - minus_side(field, which_dim))
    return result


def restrict(field):
    extent_x, extent_y, extent_z = field.shape
    return jnp.sum(field.reshape(extent_x // 2, 2, extent_y // 2, 2, extent_z // 2, 2), axis=(1, 3, 5))


def prolong(field):
    return jnp.repeat(jnp.repeat(jnp.repeat(field, 2, axis=0), 2, axis=1), 2, axis=2)


def precondition(residual, fine, coarse):
    plus_faces, minus_faces, shift_value, diagonal = fine
    coarse_plus, coarse_minus, coarse_shift, coarse_diagonal = coarse
    smooth_one = DAMPING * residual / diagonal
    coarse_rhs = restrict(residual - operate(smooth_one, plus_faces, minus_faces, shift_value))
    coarse_one = DAMPING * coarse_rhs / coarse_diagonal
    coarse_two = coarse_one + DAMPING * (coarse_rhs - operate(coarse_one, coarse_plus, coarse_minus, coarse_shift)) / coarse_diagonal
    corrected = smooth_one + prolong(coarse_two)
    return corrected + DAMPING * (residual - operate(corrected, plus_faces, minus_faces, shift_value)) / diagonal


def solve(rhs, fine, coarse):
    plus_faces, minus_faces, shift_value, diagonal = fine
    iterate = jnp.zeros_like(rhs)
    residual = rhs
    precond = precondition(residual, fine, coarse)
    gamma_now = jnp.sum(residual * precond)
    search = precond
    for turn_index in range(ITERS):
        image_field = operate(search, plus_faces, minus_faces, shift_value)
        step_length = gamma_now / jnp.sum(search * image_field)
        iterate = iterate + step_length * search
        if turn_index + 1 < ITERS:
            residual = residual - step_length * image_field
            precond = precondition(residual, fine, coarse)
            gamma_next = jnp.sum(residual * precond)
            search = precond + (gamma_next / gamma_now) * search
            gamma_now = gamma_next
    return iterate


def reference(conductivity, misfit, forward_states, pole_shifts, pole_weights, pole_order):
    plus_faces = [0.5 * (conductivity + plus_side(conductivity, which_dim)) for which_dim in range(3)]
    minus_faces = [0.5 * (conductivity + minus_side(conductivity, which_dim)) for which_dim in range(3)]
    base_diagonal = plus_faces[0] + plus_faces[1] + plus_faces[2] + minus_faces[0] + minus_faces[1] + minus_faces[2]
    coarse_plus = [coarse_pick(plus_faces[which_dim], which_dim, 1) for which_dim in range(3)]
    coarse_minus = [coarse_pick(minus_faces[which_dim], which_dim, 0) for which_dim in range(3)]
    coarse_base = coarse_plus[0] + coarse_plus[1] + coarse_plus[2] + coarse_minus[0] + coarse_minus[1] + coarse_minus[2]

    def one_slot(total, slot_items):
        state, pole = slot_items
        shift_value = pole_shifts[pole]
        weight = pole_weights[pole]
        fine = (plus_faces, minus_faces, shift_value, base_diagonal + shift_value)
        coarse = (coarse_plus, coarse_minus, 8.0 * shift_value, coarse_base + 8.0 * shift_value)
        adjoint = solve(weight * misfit, fine, coarse)
        term = jnp.zeros_like(conductivity)
        for which_dim in range(3):
            term = term + (adjoint - plus_side(adjoint, which_dim)) * (state - plus_side(state, which_dim))
            term = term + (adjoint - minus_side(adjoint, which_dim)) * (state - minus_side(state, which_dim))
        return total - 0.5 * term, adjoint

    gradient, adjoint_states = lax.scan(one_slot, jnp.zeros_like(conductivity), (forward_states, pole_order))
    return adjoint_states, gradient
```

```python
import functools

import jax
import jax.numpy as jnp
from jax import lax
from jax.experimental import pallas as pl
from jax.experimental.pallas import tpu as pltpu
from jax.sharding import PartitionSpec as P

MESH = pl.DeviceIdType.MESH
W = 0.8
NY, NZ = 64, 128
HALO = 12
PLANES = 4 + 2 * HALO


def roll(value, shift, axis):
    return pltpu.roll(value, shift % value.shape[axis], axis)


def pair_sum(value):
    value = value + roll(value, -1, 1)
    return value + roll(value, -1, 0)


def kernel(
    chips, poles,
    shift_ref, weight_ref, order_ref, kappa_ref, misfit_ref, forward_ref,
    adjoint_ref, gradient_ref,
    kap, res, face_x, face_y, face_z, diag, gain, z1, z2, u0, rt, ut,
    cgain, cface_x, cface_y, cface_z, y1,
    fwd, sib_u, sib_t, xout, part, sums, swap, term, pieces, gout,
    near_send, near_recv, sib_send, sib_recv, f_send, f_recv, loc, ar_send, ar_recv, sw_send, sw_recv,
    xs_send, xs_recv, rs_send, rs_recv,
):
    pole = lax.axis_index("pole")
    space = lax.axis_index("space")
    core = lax.rem(space, 2)
    chip = space // 2
    sibling = space + 1 - 2 * core
    steps = (1, -1, 2, -2, 3, -3)

    def has(step):
        return jnp.logical_and(chip + step >= 0, chip + step < chips)

    barrier = pltpu.get_barrier_semaphore()

    def greet(p, s):
        pl.semaphore_signal(barrier, inc=1, device_id=(p, s), device_id_type=MESH)

    def near(p_space):
        return (pole, p_space)

    greet(pole, sibling)

    def greet_chip(d, carry):
        greet(pole, lax.rem(space + 2 * d, 2 * chips))
        return carry

    lax.fori_loop(1, chips, greet_chip, 0)
    for d in range(1, poles):
        greet(lax.rem(pole + d, poles), space)
    across = space + 2 * core - 1
    has_across = jnp.logical_and(across >= 0, across < 2 * chips)

    @pl.when(has_across)
    def _():
        greet(pole, across)

    own = HALO + 2 * core
    own_copies = [
        pltpu.make_async_copy(kappa_ref, kap.at[pl.ds(own, 2)], loc.at[0]),
        pltpu.make_async_copy(misfit_ref, res.at[pl.ds(own, 2)], loc.at[1]),
        pltpu.make_async_copy(forward_ref, fwd.at[:, pl.ds(1, 2)], loc.at[2]),
    ]
    for copy in own_copies:
        copy.start()
    for step in steps:
        @pl.when(jnp.logical_not(has(step)))
        def _():
            zeros = jnp.zeros((4, NY, NZ), jnp.float32)
            kap[pl.ds(HALO + 4 * step, 4)] = zeros
            res[pl.ds(HALO + 4 * step, 4)] = zeros

    @pl.when(space == 0)
    def _():
        fwd[:, 0] = jnp.zeros((2, NY, NZ), jnp.float32)

    @pl.when(space == 2 * chips - 1)
    def _():
        fwd[:, 3] = jnp.zeros((2, NY, NZ), jnp.float32)

    pl.semaphore_wait(barrier, chips + poles - 1 + has_across.astype(jnp.int32))

    def remote(src, dst, send, recv, target):
        return pltpu.make_async_remote_copy(
            src_ref=src, dst_ref=dst, send_sem=send, recv_sem=recv,
            device_id=target, device_id_type=MESH,
        )

    def outgoing(i, step):
        at = own - 4 * step
        return [
            remote(source, dest.at[pl.ds(at, 2)], near_send.at[a, i], near_recv.at[a, i],
                   near(space + 2 * step))
            for a, (source, dest) in enumerate(((kappa_ref, kap), (misfit_ref, res)))
        ]

    def incoming(i, step):
        at = own - 4 * step
        return [
            remote(source, dest.at[pl.ds(at, 2)], near_send.at[a, i], near_recv.at[a, i],
                   near(space - 2 * step))
            for a, (source, dest) in enumerate(((kappa_ref, kap), (misfit_ref, res)))
        ]

    def passing(i, at):
        return [
            remote(dest.at[pl.ds(at, 2)], dest.at[pl.ds(at, 2)], sib_send.at[a, i], sib_recv.at[a, i],
                   near(sibling))
            for a, dest in enumerate((kap, res))
        ]

    def taken(i, at):
        return [
            remote(dest.at[pl.ds(at, 2)], dest.at[pl.ds(at, 2)], sib_send.at[a, i], sib_recv.at[a, i],
                   near(sibling))
            for a, dest in enumerate((kap, res))
        ]

    for i, step in enumerate(steps):
        @pl.when(has(step))
        def _():
            for copy in outgoing(i, step):
                copy.start()

    for copy in own_copies:
        copy.wait()
    for copy in passing(6, own):
        copy.start()

    previous, following = space - 1, space + 1
    to_previous = remote(forward_ref.at[:, 0], fwd.at[:, 3], f_send.at[0], f_recv.at[0], near(previous))
    to_following = remote(forward_ref.at[:, 1], fwd.at[:, 0], f_send.at[1], f_recv.at[1], near(following))

    @pl.when(space > 0)
    def _():
        to_previous.start()

    @pl.when(space < 2 * chips - 1)
    def _():
        to_following.start()

    for i, step in enumerate(steps):
        @pl.when(has(-step))
        def _():
            for copy in incoming(i, step):
                copy.wait_recv()
            for copy in passing(i, own - 4 * step):
                copy.start()

    other = HALO + 2 * (1 - core)
    for copy in taken(6, other):
        copy.wait_recv()
    for i, step in enumerate(steps):
        @pl.when(has(-step))
        def _():
            for copy in taken(i, other - 4 * step):
                copy.wait_recv()

    pole_here = order_ref[core]
    shift = shift_ref[pole_here]
    weight = weight_ref[pole_here]

    row = lax.broadcasted_iota(jnp.int32, (NY, NZ), 0)
    col = lax.broadcasted_iota(jnp.int32, (NY, NZ), 1)
    row_first, row_last = row == 0, row == NY - 1
    col_first, col_last = col == 0, col == NZ - 1
    row_odd, col_odd = lax.rem(row, 2) == 1, lax.rem(col, 2) == 1

    def inside(i):
        plane = 4 * chip + i - HALO
        return jnp.logical_and(plane >= 0, plane < 4 * chips)

    def fine_faces(i, odd):
        k = kap[i]
        fx, bx = 0.5 * (k + kap[i + 1]), 0.5 * (k + kap[i - 1])
        up_y = jnp.where(row_last, 0.0, roll(k, -1, 0))
        down_y = jnp.where(row_first, 0.0, roll(k, 1, 0))
        up_z = jnp.where(col_last, 0.0, roll(k, -1, 1))
        down_z = jnp.where(col_first, 0.0, roll(k, 1, 1))
        py, qy = 0.5 * (k + up_y), 0.5 * (k + down_y)
        pz, qz = 0.5 * (k + up_z), 0.5 * (k + down_z)
        d = shift + (fx + bx + (py + qy) + (pz + qz))
        g = jnp.where(inside(i), W, 0.0) / d
        my, mz = jnp.where(row_last, 0.0, py), jnp.where(col_last, 0.0, pz)
        face_x[i] = fx
        face_y[i] = my
        face_z[i] = mz
        diag[i] = d
        gain[i] = g
        z1[i] = g * res[i]
        block = shift + (fx if odd else bx) + jnp.where(row_odd, py, qy) + jnp.where(col_odd, pz, qz)
        return fx, block, jnp.where(row_odd, my, 0.0), jnp.where(col_odd, mz, 0.0)

    face_x[0] = 0.5 * (kap[0] + kap[1])
    fine_faces(1, True)
    fine_faces(PLANES - 2, False)

    def faces(j, carry):
        i = 2 * j
        _, block0, fy0, fz0 = fine_faces(i, False)
        fx, block1, fy1, fz1 = fine_faces(i + 1, True)
        cface_x[j] = pair_sum(fx)
        cface_y[j] = pair_sum(fy0 + fy1)
        cface_z[j] = pair_sum(fz0 + fz1)
        cgain[j] = jnp.where(inside(i), W, 0.0) / pair_sum(block0 + block1)
        return carry

    lax.fori_loop(1, PLANES // 2 - 1, faces, 0)

    def off(ref, i):
        v = ref[i]
        fy, fz = face_y[i], face_z[i]
        total = face_x[i] * ref[i + 1] + face_x[i - 1] * ref[i - 1]
        total = total + (fy * roll(v, -1, 0) + roll(fy * v, 1, 0))
        return total + (fz * roll(v, -1, 1) + roll(fz * v, 1, 1))

    def coarse_off(j):
        v = y1[j]
        fy, fz = cface_y[j], cface_z[j]
        total = cface_x[j] * y1[j + 1] + cface_x[j - 1] * y1[j - 1]
        total = total + (fy * roll(v, -2, 0) + roll(fy * v, 2, 0))
        return total + (fz * roll(v, -2, 1) + roll(fz * v, 2, 1))

    def precondition(source, out, lo, hi):
        def down(j, carry):
            i = 2 * j
            t = 0.2 * (source[i] + source[i + 1]) + (off(z1, i) + off(z1, i + 1))
            y1[j] = cgain[j] * pair_sum(t)
            return carry

        def up(j, carry):
            i = 2 * j
            y2 = 1.2 * y1[j] + cgain[j] * coarse_off(j)
            y2 = jnp.where(col_odd, roll(y2, 1, 1), y2)
            y2 = jnp.where(row_odd, roll(y2, 1, 0), y2)
            z2[i] = z1[i] + y2
            z2[i + 1] = z1[i + 1] + y2
            return carry

        def smooth(i, carry):
            out[i] = 0.2 * z2[i] + z1[i] + gain[i] * off(z2, i)
            return carry

        first, last = (lo - 1) // 2, hi // 2
        lax.fori_loop(first - 1, last + 2, down, 0)
        lax.fori_loop(first, last + 1, up, 0)
        lax.fori_loop(lo, hi, smooth, 0)

    precondition(res, u0, HALO - 6, HALO + 10)

    def residual(i, carry):
        value = res[i] - (diag[i] * u0[i] - off(u0, i))
        rt[i] = value
        z1[i] = gain[i] * value
        return carry

    lax.fori_loop(HALO - 5, HALO + 9, residual, 0)
    precondition(rt, ut, HALO - 1, HALO + 5)

    window = HALO - 1 + 2 * core
    sib_window = HALO + 1 - 2 * core
    swaps = [
        remote(u0.at[pl.ds(sib_window, 4)], sib_u, xs_send.at[0], xs_recv.at[0], near(sibling)),
        remote(ut.at[pl.ds(sib_window, 4)], sib_t, xs_send.at[1], xs_recv.at[1], near(sibling)),
    ]
    for copy in swaps:
        copy.start()

    def products(i, carry):
        g0, d0, e1, m0 = carry
        u, t, r, q = u0[i], rt[i], res[i], ut[i]
        image = diag[i] * q - off(ut, i)
        fold = lambda v: jnp.sum(v.reshape(NY // 8, 8, NZ), axis=0)
        return (g0 + fold(u * r), d0 + fold(u * t), e1 + fold(t * q), m0 + fold(q * image))

    zero = jnp.zeros((8, NZ), jnp.float32)
    totals = lax.fori_loop(HALO, HALO + 4, products, (zero,) * 4)
    sub = lax.broadcasted_iota(jnp.int32, (8, NZ), 0)
    tile = zero
    for k, total in enumerate(totals):
        tile = jnp.where(sub == k, jnp.sum(total, axis=0, keepdims=True), tile)
    part[0] = tile

    def reduce_copy(d):
        return remote(part.at[0], part.at[d], ar_send, ar_recv,
                      near(lax.rem(space + 2 * d, 2 * chips)))

    def reduce_start(d, carry):
        reduce_copy(d).start()
        return carry

    lax.fori_loop(1, chips, reduce_start, 0)
    everyone = pltpu.make_async_copy(part.at[pl.ds(1, chips - 1)], part.at[pl.ds(1, chips - 1)], ar_recv)
    everyone.wait()
    total = jnp.sum(part[...], axis=0)
    total = jnp.sum(total, axis=1, keepdims=True)
    lane = lax.broadcasted_iota(jnp.int32, (8, NZ), 1)

    g0, d0, e1, m0 = (total[k : k + 1] for k in range(4))
    c0 = g0 - d0
    eta = d0 / c0
    a0 = 1.0 + eta
    t = d0 - e1
    k = c0 - t
    g1 = e1 - 2.0 * eta * t + eta * eta * k
    b = g1 / g0
    s11 = m0 - 2.0 * eta * (t - m0) + eta * eta * (k - t + m0)
    c1 = s11 + 2.0 * b * (t - eta * k) + b * b * c0
    a1 = g1 / c1
    first = weight * (a0 + a1 * (b - eta))
    second = weight * (a1 * a0)
    sums[...] = jnp.where(lane == 0, first, second)
    scalars = remote(sums, swap, sw_send, sw_recv, near(sibling))
    scalars.start()
    for copy in swaps:
        copy.wait_recv()

    def combine(source_u, source_t, at, slot, one, two):
        for n in range(4):
            xout[slot, n] = one * source_u[at + n] + two * source_t[at + n]

    combine(u0, ut, window, core, first, second)
    scalars.wait_recv()
    combine(sib_u, sib_t, 0, 1 - core, swap[0:1, 0:1], swap[0:1, 1:2])
    adjoint_out = pltpu.make_async_copy(xout.at[:, pl.ds(1, 2)], adjoint_ref, loc.at[3])
    adjoint_out.start()

    @pl.when(space > 0)
    def _():
        to_following.wait_recv()

    @pl.when(space < 2 * chips - 1)
    def _():
        to_previous.wait_recv()

    def side(x, f, axis, first_mask, last_mask):
        forward = (x - jnp.where(last_mask, 0.0, roll(x, -1, axis))) * (
            f - jnp.where(last_mask, 0.0, roll(f, -1, axis))
        )
        return forward + jnp.where(first_mask, x * f, roll(forward, 1, axis))

    def terms(n, carry):
        total = jnp.zeros((NY, NZ), jnp.float32)
        for slot in range(2):
            x, f = xout[slot, n], fwd[slot, n]
            total = total + (x - xout[slot, n + 1]) * (f - fwd[slot, n + 1])
            total = total + (x - xout[slot, n - 1]) * (f - fwd[slot, n - 1])
            total = total + side(x, f, 0, row_first, row_last) + side(x, f, 1, col_first, col_last)
        term[n - 1] = -0.5 * total
        return carry

    lax.fori_loop(1, 3, terms, 0)

    def rows(q):
        return term.at[:, pl.ds(pl.multiple_of(8 * q, 8), 8), :]

    spread = []
    for d in range(1, poles):
        q = lax.rem(pole + d, poles)
        spread.append(remote(rows(q), pieces.at[d], rs_send.at[d], rs_recv.at[d], (q, space)))
    for copy in spread:
        copy.start()
    total = term[:, pl.ds(pl.multiple_of(8 * pole, 8), 8), :]
    for d, copy in enumerate(spread):
        copy.wait_recv()
        total = total + pieces[d + 1]
    gout[...] = total
    gradient_out = pltpu.make_async_copy(gout, gradient_ref, loc.at[4])
    gradient_out.start()

    for i, step in enumerate(steps):
        @pl.when(has(step))
        def _():
            for copy in outgoing(i, step):
                copy.wait_send()

        @pl.when(has(-step))
        def _():
            for copy in passing(i, own - 4 * step):
                copy.wait_send()
    for copy in passing(6, own):
        copy.wait_send()

    @pl.when(space > 0)
    def _():
        to_previous.wait_send()

    @pl.when(space < 2 * chips - 1)
    def _():
        to_following.wait_send()

    for copy in swaps:
        copy.wait_send()
    pltpu.make_async_copy(part.at[pl.ds(1, chips - 1)], part.at[pl.ds(1, chips - 1)], ar_send).wait()
    scalars.wait_send()
    for copy in spread:
        copy.wait_send()
    adjoint_out.wait()
    gradient_out.wait()


def solution(mesh):
    chips, poles = mesh.shape["space"] // 2, mesh.shape["pole"]
    f32 = jnp.float32

    def per_device(conductivity, misfit, forward_states, pole_shifts, pole_weights, pole_order):
        smem = pl.BlockSpec(memory_space=pltpu.SMEM)
        hbm = pl.BlockSpec(memory_space=pl.ANY)
        fine = pltpu.VMEM((PLANES, NY, NZ), f32)
        coarse = pltpu.VMEM((PLANES // 2, NY, NZ), f32)
        window = pltpu.VMEM((4, NY, NZ), f32)
        dma = pltpu.SemaphoreType.DMA
        return pl.pallas_call(
            functools.partial(kernel, chips, poles),
            out_shape=(
                jax.ShapeDtypeStruct(forward_states.shape, f32),
                jax.ShapeDtypeStruct((2, NY // poles, NZ), f32),
            ),
            in_specs=[smem, smem, smem, hbm, hbm, hbm],
            out_specs=(hbm, hbm),
            scratch_shapes=[fine] * 12 + [coarse] * 5 + [
                pltpu.VMEM((2, 4, NY, NZ), f32), window, window, pltpu.VMEM((2, 4, NY, NZ), f32),
                pltpu.VMEM((chips, 8, NZ), f32), pltpu.VMEM((8, NZ), f32), pltpu.VMEM((8, NZ), f32),
                pltpu.VMEM((2, NY, NZ), f32), pltpu.VMEM((poles, 2, NY // poles, NZ), f32),
                pltpu.VMEM((2, NY // poles, NZ), f32),
                dma((2, 6)), dma((2, 6)), dma((2, 7)), dma((2, 7)), dma((2,)), dma((2,)), dma((5,)),
                dma, dma, dma, dma, dma((2,)), dma((2,)), dma((poles,)), dma((poles,)),
            ],
            compiler_params=pltpu.CompilerParams(
                collective_id=0, has_side_effects=True, vmem_limit_bytes=40 << 20
            ),
            name="adjoint_gradient",
        )(pole_shifts, pole_weights, pole_order, conductivity, misfit, forward_states)

    in_specs = (
        P("space", None, None), P("space", None, None), P("pole", "space", None, None),
        P(), P(), P("pole"),
    )
    out_specs = (P("pole", "space", None, None), P("space", "pole", None))
    return jax.shard_map(per_device, mesh=mesh, in_specs=in_specs, out_specs=out_specs, check_vma=False)
```

```python
import functools

import jax
import jax.numpy as jnp
from jax import lax
from jax.experimental import pallas as pl
from jax.experimental.pallas import tpu as pltpu
from jax.sharding import PartitionSpec as P

MESH = pl.DeviceIdType.MESH
W = 0.8
UNROLL_F, UNROLL_D, UNROLL_U, UNROLL_S, UNROLL_R = 4, True, True, True, True
NY, NZ = 64, 128
HALO = 12
PLANES = 4 + 2 * HALO


def roll(value, shift, axis):
    return pltpu.roll(value, shift % value.shape[axis], axis)


def next_row(value):
    return jnp.concatenate([value[1:], roll(value[:1], -1, 1)], axis=0)


def previous_row(value):
    return jnp.concatenate([roll(value[-1:], 1, 1), value[:-1]], axis=0)


def rows_of(value):
    pairs = value.reshape(value.shape[0] // 2, 2, *value.shape[1:])
    return pairs[:, 0], pairs[:, 1]


def row_pairs(value):
    even, odd = rows_of(value)
    return even + odd


def pair_sum(value):
    value = row_pairs(value)
    return value + roll(value, -1, 2)


def natural(ref, index):
    return jnp.stack([ref[(*index, pl.ds(v, 8, stride=8), slice(None))] for v in range(8)])


def put_natural(ref, index, value):
    for v in range(8):
        ref[(*index, pl.ds(v, 8, stride=8), slice(None))] = value[v]


def kernel(
    chips, poles,
    shift_ref, weight_ref, order_ref, kappa_ref, misfit_ref, forward_ref,
    adjoint_ref, gradient_ref,
    shift_mem, weight_mem, order_mem, kap, res, face_x, face_y, face_z, diag, gain, z1, z2, u0, rt, ut,
    cgain, cface_x, cface_y, cface_z, y1,
    stage, fwd, sib_u, sib_t, xout, xnat, part, sums, swap, term, pieces, gout,
    near_send, near_recv, sib_send, sib_recv, f_send, f_recv, loc, ar_send, ar_recv, sw_send, sw_recv,
    xs_send, xs_recv, rs_send, rs_recv,
):
    pole = lax.axis_index("pole")
    space = lax.axis_index("space")
    core = lax.rem(space, 2)
    chip = space // 2
    sibling = space + 1 - 2 * core
    steps = (1, -1, 2, -2, 3, -3)

    def has(step):
        return jnp.logical_and(chip + step >= 0, chip + step < chips)

    barrier = pltpu.get_barrier_semaphore()

    def greet(p, s):
        pl.semaphore_signal(barrier, inc=1, device_id=(p, s), device_id_type=MESH)

    def near(p_space):
        return (pole, p_space)

    greet(pole, sibling)

    def greet_chip(d, carry):
        greet(pole, lax.rem(space + 2 * d, 2 * chips))
        return carry

    lax.fori_loop(1, chips, greet_chip, 0)
    for d in range(1, poles):
        greet(lax.rem(pole + d, poles), space)
    across = space + 2 * core - 1
    has_across = jnp.logical_and(across >= 0, across < 2 * chips)

    @pl.when(has_across)
    def _():
        greet(pole, across)

    own = HALO + 2 * core
    own_copies = [
        pltpu.make_async_copy(kappa_ref, stage.at[0], loc.at[0]),
        pltpu.make_async_copy(misfit_ref, stage.at[1], loc.at[1]),
        pltpu.make_async_copy(forward_ref, stage.at[pl.ds(2, 2)], loc.at[2]),
        pltpu.make_async_copy(shift_ref, shift_mem, loc.at[3]),
        pltpu.make_async_copy(weight_ref, weight_mem, loc.at[4]),
        pltpu.make_async_copy(order_ref, order_mem, loc.at[5]),
    ]
    for copy in own_copies:
        copy.start()
    for step in steps:
        @pl.when(jnp.logical_not(has(step)))
        def _():
            zeros = jnp.zeros((4, 8, 8, NZ), jnp.float32)
            kap[pl.ds(HALO + 4 * step, 4)] = zeros
            res[pl.ds(HALO + 4 * step, 4)] = zeros

    @pl.when(space == 0)
    def _():
        fwd[:, 0] = jnp.zeros((2, 8, 8, NZ), jnp.float32)

    @pl.when(space == 2 * chips - 1)
    def _():
        fwd[:, 3] = jnp.zeros((2, 8, 8, NZ), jnp.float32)

    for copy in own_copies:
        copy.wait()
    for n in range(2):
        kap[own + n] = natural(stage, (0, n))
        res[own + n] = natural(stage, (1, n))
        for slot in range(2):
            fwd[slot, 1 + n] = natural(stage, (2 + slot, n))

    pl.semaphore_wait(barrier, chips + poles - 1 + has_across.astype(jnp.int32))

    def remote(src, dst, send, recv, target):
        return pltpu.make_async_remote_copy(
            src_ref=src, dst_ref=dst, send_sem=send, recv_sem=recv,
            device_id=target, device_id_type=MESH,
        )

    def outgoing(i, step):
        at = own - 4 * step
        return [
            remote(dest.at[pl.ds(own, 2)], dest.at[pl.ds(at, 2)], near_send.at[a, i], near_recv.at[a, i],
                   near(space + 2 * step))
            for a, dest in enumerate((kap, res))
        ]

    def incoming(i, step):
        at = own - 4 * step
        return [
            remote(dest.at[pl.ds(own, 2)], dest.at[pl.ds(at, 2)], near_send.at[a, i], near_recv.at[a, i],
                   near(space - 2 * step))
            for a, dest in enumerate((kap, res))
        ]

    def passing(i, at):
        return [
            remote(dest.at[pl.ds(at, 2)], dest.at[pl.ds(at, 2)], sib_send.at[a, i], sib_recv.at[a, i],
                   near(sibling))
            for a, dest in enumerate((kap, res))
        ]

    def taken(i, at):
        return [
            remote(dest.at[pl.ds(at, 2)], dest.at[pl.ds(at, 2)], sib_send.at[a, i], sib_recv.at[a, i],
                   near(sibling))
            for a, dest in enumerate((kap, res))
        ]

    for i, step in enumerate(steps):
        @pl.when(has(step))
        def _():
            for copy in outgoing(i, step):
                copy.start()

    for copy in passing(6, own):
        copy.start()

    previous, following = space - 1, space + 1
    to_previous = remote(fwd.at[:, 1], fwd.at[:, 3], f_send.at[0], f_recv.at[0], near(previous))
    to_following = remote(fwd.at[:, 2], fwd.at[:, 0], f_send.at[1], f_recv.at[1], near(following))

    @pl.when(space > 0)
    def _():
        to_previous.start()

    @pl.when(space < 2 * chips - 1)
    def _():
        to_following.start()

    for i, step in enumerate(steps):
        @pl.when(has(-step))
        def _():
            for copy in incoming(i, step):
                copy.wait_recv()
            for copy in passing(i, own - 4 * step):
                copy.start()

    other = HALO + 2 * (1 - core)
    for copy in taken(6, other):
        copy.wait_recv()
    for i, step in enumerate(steps):
        @pl.when(has(-step))
        def _():
            for copy in taken(i, other - 4 * step):
                copy.wait_recv()

    pole_here = order_mem[core]
    shift = shift_mem[pole_here]
    weight = weight_mem[pole_here]

    block = (8, 8, NZ)
    row = 8 * lax.broadcasted_iota(jnp.int32, block, 1) + lax.broadcasted_iota(jnp.int32, block, 0)
    col = lax.broadcasted_iota(jnp.int32, block, 2)
    row_first, row_last = row == 0, row == NY - 1
    col_first, col_last = col == 0, col == NZ - 1
    col_odd = lax.rem(lax.broadcasted_iota(jnp.int32, (4, 8, NZ), 2), 2) == 1

    def inside(i):
        plane = 4 * chip + i - HALO
        return jnp.logical_and(plane >= 0, plane < 4 * chips)

    def fine_faces(i, odd):
        k = kap[i]
        fx, bx = 0.5 * (k + kap[i + 1]), 0.5 * (k + kap[i - 1])
        up_y = jnp.where(row_last, 0.0, next_row(k))
        down_y = jnp.where(row_first, 0.0, previous_row(k))
        up_z = jnp.where(col_last, 0.0, roll(k, -1, 2))
        down_z = jnp.where(col_first, 0.0, roll(k, 1, 2))
        py, qy = 0.5 * (k + up_y), 0.5 * (k + down_y)
        pz, qz = 0.5 * (k + up_z), 0.5 * (k + down_z)
        d = shift + (fx + bx + (py + qy) + (pz + qz))
        g = jnp.where(inside(i), W, 0.0) / d
        my, mz = jnp.where(row_last, 0.0, py), jnp.where(col_last, 0.0, pz)
        face_x[i] = fx
        face_y[i] = my
        face_z[i] = mz
        diag[i] = d
        gain[i] = g
        z1[i] = g * res[i]
        around = row_pairs(shift + (fx if odd else bx)), rows_of(qy)[0] + rows_of(py)[1], row_pairs(pz), row_pairs(qz)
        return fx, around, rows_of(my)[1], row_pairs(mz)

    face_x[0] = 0.5 * (kap[0] + kap[1])
    fine_faces(1, True)
    fine_faces(PLANES - 2, False)

    def faces(j, carry):
        i = 2 * j
        _, (bx0, by0, pz0, qz0), fy0, fz0 = fine_faces(i, False)
        fx, (bx1, by1, pz1, qz1), fy1, fz1 = fine_faces(i + 1, True)
        cface_x[j] = pair_sum(fx)
        fy = fy0 + fy1
        cface_y[j] = fy + roll(fy, -1, 2)
        cface_z[j] = roll(fz0 + fz1, -1, 2)
        both = (bx0 + bx1) + (by0 + by1)
        d = both + (qz0 + qz1) + roll(both + (pz0 + pz1), -1, 2)
        cgain[j] = jnp.where(inside(i), W, 0.0) / d
        return carry

    lax.fori_loop(1, PLANES // 2 - 1, faces, 0, unroll=UNROLL_F)

    def off(ref, i):
        v = ref[i]
        fy, fz = face_y[i], face_z[i]
        total = face_x[i] * ref[i + 1] + face_x[i - 1] * ref[i - 1]
        total = total + (fy * next_row(v) + previous_row(fy * v))
        return total + (fz * roll(v, -1, 2) + roll(fz * v, 1, 2))

    def coarse_off(j):
        v = y1[j]
        fy, fz = cface_y[j], cface_z[j]
        total = cface_x[j] * y1[j + 1] + cface_x[j - 1] * y1[j - 1]
        total = total + (fy * next_row(v) + previous_row(fy * v))
        return total + (fz * roll(v, -2, 2) + roll(fz * v, 2, 2))

    def precondition(source, out, lo, hi):
        def down(j, carry):
            i = 2 * j
            t = 0.2 * (source[i] + source[i + 1]) + (off(z1, i) + off(z1, i + 1))
            y1[j] = cgain[j] * pair_sum(t)
            return carry

        def up(j, carry):
            i = 2 * j
            y2 = 1.2 * y1[j] + cgain[j] * coarse_off(j)
            y2 = jnp.where(col_odd, roll(y2, 1, 2), y2)
            y2 = jnp.stack([y2, y2], axis=1).reshape(8, 8, NZ)
            z2[i] = z1[i] + y2
            z2[i + 1] = z1[i + 1] + y2
            return carry

        def smooth(i, carry):
            out[i] = 0.2 * z2[i] + z1[i] + gain[i] * off(z2, i)
            return carry

        first, last = (lo - 1) // 2, hi // 2
        lax.fori_loop(first - 1, last + 2, down, 0, unroll=UNROLL_D)
        lax.fori_loop(first, last + 1, up, 0, unroll=UNROLL_U)
        lax.fori_loop(lo, hi, smooth, 0, unroll=UNROLL_S)

    precondition(res, u0, HALO - 6, HALO + 10)

    def residual(i, carry):
        value = res[i] - (diag[i] * u0[i] - off(u0, i))
        rt[i] = value
        z1[i] = gain[i] * value
        return carry

    lax.fori_loop(HALO - 5, HALO + 9, residual, 0, unroll=UNROLL_R)
    precondition(rt, ut, HALO - 1, HALO + 5)

    window = HALO - 1 + 2 * core
    sib_window = HALO + 1 - 2 * core
    swaps = [
        remote(u0.at[pl.ds(sib_window, 4)], sib_u, xs_send.at[0], xs_recv.at[0], near(sibling)),
        remote(ut.at[pl.ds(sib_window, 4)], sib_t, xs_send.at[1], xs_recv.at[1], near(sibling)),
    ]
    for copy in swaps:
        copy.start()

    def products(i, carry):
        g0, d0, e1, m0 = carry
        u, t, r, q = u0[i], rt[i], res[i], ut[i]
        image = diag[i] * q - off(ut, i)
        fold = lambda v: jnp.sum(v, axis=0)
        return (g0 + fold(u * r), d0 + fold(u * t), e1 + fold(t * q), m0 + fold(q * image))

    zero = jnp.zeros((8, NZ), jnp.float32)
    totals = lax.fori_loop(HALO, HALO + 4, products, (zero,) * 4)
    sub = lax.broadcasted_iota(jnp.int32, (8, NZ), 0)
    tile = zero
    for k, total in enumerate(totals):
        tile = jnp.where(sub == k, jnp.sum(total, axis=0, keepdims=True), tile)
    part[0] = tile

    def reduce_copy(d):
        return remote(part.at[0], part.at[d], ar_send, ar_recv,
                      near(lax.rem(space + 2 * d, 2 * chips)))

    def reduce_start(d, carry):
        reduce_copy(d).start()
        return carry

    lax.fori_loop(1, chips, reduce_start, 0)
    everyone = pltpu.make_async_copy(part.at[pl.ds(1, chips - 1)], part.at[pl.ds(1, chips - 1)], ar_recv)
    everyone.wait()
    total = jnp.sum(part[...], axis=0)
    total = jnp.sum(total, axis=1, keepdims=True)
    lane = lax.broadcasted_iota(jnp.int32, (8, NZ), 1)

    g0, d0, e1, m0 = (total[k : k + 1] for k in range(4))
    c0 = g0 - d0
    eta = d0 / c0
    a0 = 1.0 + eta
    t = d0 - e1
    k = c0 - t
    g1 = e1 - 2.0 * eta * t + eta * eta * k
    b = g1 / g0
    s11 = m0 - 2.0 * eta * (t - m0) + eta * eta * (k - t + m0)
    c1 = s11 + 2.0 * b * (t - eta * k) + b * b * c0
    a1 = g1 / c1
    first = weight * (a0 + a1 * (b - eta))
    second = weight * (a1 * a0)
    sums[...] = jnp.where(lane == 0, first, second)
    scalars = remote(sums, swap, sw_send, sw_recv, near(sibling))
    scalars.start()
    for copy in swaps:
        copy.wait_recv()

    def combine(source_u, source_t, at, slot, one, two):
        for n in range(4):
            xout[slot, n] = one * source_u[at + n] + two * source_t[at + n]

    combine(u0, ut, window, core, first, second)
    scalars.wait_recv()
    combine(sib_u, sib_t, 0, 1 - core, swap[0:1, 0:1], swap[0:1, 1:2])
    for slot in range(2):
        for n in range(2):
            put_natural(xnat, (slot, n), xout[slot, 1 + n])
    adjoint_out = pltpu.make_async_copy(xnat, adjoint_ref, loc.at[3])
    adjoint_out.start()

    @pl.when(space > 0)
    def _():
        to_following.wait_recv()

    @pl.when(space < 2 * chips - 1)
    def _():
        to_previous.wait_recv()

    def ahead_row(v):
        return jnp.where(row_last, 0.0, next_row(v))

    def ahead_col(v):
        return jnp.where(col_last, 0.0, roll(v, -1, 2))

    def terms(n, carry):
        total = jnp.zeros(block, jnp.float32)
        for slot in range(2):
            x, f = xout[slot, n], fwd[slot, n]
            total = total + (x - xout[slot, n + 1]) * (f - fwd[slot, n + 1])
            total = total + (x - xout[slot, n - 1]) * (f - fwd[slot, n - 1])
            product = x * f
            ahead = (x - ahead_row(x)) * (f - ahead_row(f))
            total = total + ahead + jnp.where(row_first, product, previous_row(ahead))
            ahead = (x - ahead_col(x)) * (f - ahead_col(f))
            total = total + ahead + jnp.where(col_first, product, roll(ahead, 1, 2))
        put_natural(term, (n - 1,), -0.5 * total)
        return carry

    lax.fori_loop(1, 3, terms, 0)

    def rows(q):
        return term.at[:, pl.ds(pl.multiple_of(8 * q, 8), 8), :]

    spread = []
    for d in range(1, poles):
        q = lax.rem(pole + d, poles)
        spread.append(remote(rows(q), pieces.at[d], rs_send.at[d], rs_recv.at[d], (q, space)))
    for copy in spread:
        copy.start()
    total = term[:, pl.ds(pl.multiple_of(8 * pole, 8), 8), :]
    for d, copy in enumerate(spread):
        copy.wait_recv()
        total = total + pieces[d + 1]
    gout[...] = total
    gradient_out = pltpu.make_async_copy(gout, gradient_ref, loc.at[4])
    gradient_out.start()

    for i, step in enumerate(steps):
        @pl.when(has(step))
        def _():
            for copy in outgoing(i, step):
                copy.wait_send()

        @pl.when(has(-step))
        def _():
            for copy in passing(i, own - 4 * step):
                copy.wait_send()
    for copy in passing(6, own):
        copy.wait_send()

    @pl.when(space > 0)
    def _():
        to_previous.wait_send()

    @pl.when(space < 2 * chips - 1)
    def _():
        to_following.wait_send()

    for copy in swaps:
        copy.wait_send()
    pltpu.make_async_copy(part.at[pl.ds(1, chips - 1)], part.at[pl.ds(1, chips - 1)], ar_send).wait()
    scalars.wait_send()
    for copy in spread:
        copy.wait_send()
    adjoint_out.wait()
    gradient_out.wait()


def solution(mesh):
    chips, poles = mesh.shape["space"] // 2, mesh.shape["pole"]
    f32 = jnp.float32

    def per_device(conductivity, misfit, forward_states, pole_shifts, pole_weights, pole_order):
        hbm = pl.BlockSpec(memory_space=pltpu.HBM)
        fine = pltpu.VMEM((PLANES, 8, 8, NZ), f32)
        coarse = pltpu.VMEM((PLANES // 2, 4, 8, NZ), f32)
        window = pltpu.VMEM((4, 8, 8, NZ), f32)
        windows = pltpu.VMEM((2, 4, 8, 8, NZ), f32)
        dma = pltpu.SemaphoreType.DMA
        return pl.pallas_call(
            functools.partial(kernel, chips, poles),
            out_shape=(
                jax.ShapeDtypeStruct(forward_states.shape, f32),
                jax.ShapeDtypeStruct((2, NY // poles, NZ), f32),
            ),
            in_specs=[hbm] * 6,
            out_specs=(hbm, hbm),
            scratch_shapes=[pltpu.SMEM(pole_shifts.shape, f32), pltpu.SMEM(pole_weights.shape, f32),
                            pltpu.SMEM(pole_order.shape, jnp.int32)]
            + [fine] * 12 + [coarse] * 5 + [
                pltpu.VMEM((4, 2, NY, NZ), f32), windows, window, window, windows,
                pltpu.VMEM((2, 2, NY, NZ), f32),
                pltpu.VMEM((chips, 8, NZ), f32), pltpu.VMEM((8, NZ), f32), pltpu.VMEM((8, NZ), f32),
                pltpu.VMEM((2, NY, NZ), f32), pltpu.VMEM((poles, 2, NY // poles, NZ), f32),
                pltpu.VMEM((2, NY // poles, NZ), f32),
                dma((2, 6)), dma((2, 6)), dma((2, 7)), dma((2, 7)), dma((2,)), dma((2,)), dma((6,)),
                dma, dma, dma, dma, dma((2,)), dma((2,)), dma((poles,)), dma((poles,)),
            ],
            compiler_params=pltpu.CompilerParams(
                collective_id=0, has_side_effects=True, vmem_limit_bytes=64 << 20
            ),
            name="adjoint_gradient",
        )(pole_shifts, pole_weights, pole_order, conductivity, misfit, forward_states)

    in_specs = (
        P("space", None, None), P("space", None, None), P("pole", "space", None, None),
        P(), P(), P("pole"),
    )
    out_specs = (P("pole", "space", None, None), P("space", "pole", None))
    return jax.shard_map(per_device, mesh=mesh, in_specs=in_specs, out_specs=out_specs, check_vma=False)
```

```python
import functools

import jax
import jax.numpy as jnp
from jax import lax
from jax.experimental import pallas as pl
from jax.experimental.pallas import tpu as pltpu
from jax.sharding import PartitionSpec as P

MESH = pl.DeviceIdType.MESH
W = 0.8
NY, NZ = 64, 128
HALO = 12
PLANES = 4 + 2 * HALO
TOKENS = (3, 6, 12, 24)
TOP = NY // 2 + 8


def roll(value, shift, axis):
    return pltpu.roll(value, shift % value.shape[axis], axis)


def next_row(value):
    return jnp.concatenate([value[1:], roll(value[:1], -1, 1)], axis=0)


def previous_row(value):
    return jnp.concatenate([roll(value[-1:], 1, 1), value[:-1]], axis=0)


def rows_of(value):
    pairs = value.reshape(value.shape[0] // 2, 2, *value.shape[1:])
    return pairs[:, 0], pairs[:, 1]


def row_pairs(value):
    even, odd = rows_of(value)
    return even + odd


def pair_sum(value):
    value = row_pairs(value)
    return value + roll(value, -1, 2)


def lane_sides(value, shifts):
    rows = value.reshape(-1, NZ)
    high = rows.astype(jnp.bfloat16)
    rest = rows - high.astype(jnp.float32)
    mid = rest.astype(jnp.bfloat16)
    low = (rest - mid.astype(jnp.float32)).astype(jnp.bfloat16)
    out = jnp.dot(jnp.concatenate([high, mid, low], axis=1), shifts, preferred_element_type=jnp.float32)
    return out[:, :NZ].reshape(value.shape), out[:, NZ:].reshape(value.shape)


def natural(ref, index):
    return jnp.stack([ref[(*index, pl.ds(v, 8, stride=8), slice(None))] for v in range(8)])


def put_natural(ref, index, value):
    for v in range(8):
        ref[(*index, pl.ds(v, 8, stride=8), slice(None))] = value[v]


def kernel(
    chips, poles,
    shift_ref, weight_ref, order_ref, kappa_ref, misfit_ref, forward_ref,
    adjoint_ref, gradient_ref,
    shift_mem, weight_mem, order_mem,
    kap, res, face_x, face_y, face_z, down_z, base, diag, gain, z1, z2, rt,
    cface_x, cface_y, cface_z, cbase, cgain, y1, u0, ut,
    sib_u, sib_t, fwd, xout, stage, stage_far, xnat, term, param, part, sums, swap, pieces, gout, gfar, gnear, shifts,
    loc, near_send, near_recv, sib_send, sib_recv, f_send, f_recv, ar_send, ar_recv, sw_send, sw_recv,
    xs_send, xs_recv, rs_send, rs_recv, far_send, far_recv, token,
):
    half_poles = poles // 2
    pole = lax.axis_index("pole")
    space = lax.axis_index("space")
    half, yy = pole // half_poles, lax.rem(pole, half_poles)
    early, late = half == 0, half == 1
    partner = lax.rem(pole + half_poles, poles)
    core = lax.rem(space, 2)
    chip = space // 2
    sibling = space + 1 - 2 * core
    has_previous, has_following = space > 0, space < 2 * chips - 1
    steps = (1, -1, 2, -2, 3, -3)

    def has(step):
        return jnp.logical_and(chip + step >= 0, chip + step < chips)

    own = HALO + 2 * core
    own_copies = [
        pltpu.make_async_copy(kappa_ref, stage.at[0], loc.at[0]),
        pltpu.make_async_copy(misfit_ref, stage.at[1], loc.at[1]),
        pltpu.make_async_copy(forward_ref, stage.at[pl.ds(2, 2)], loc.at[2]),
        pltpu.make_async_copy(shift_ref, shift_mem, loc.at[3]),
        pltpu.make_async_copy(weight_ref, weight_mem, loc.at[4]),
        pltpu.make_async_copy(order_ref, order_mem, loc.at[5]),
    ]
    for copy in own_copies:
        copy.start()

    barrier = pltpu.get_barrier_semaphore()

    def greet(p, s):
        pl.semaphore_signal(barrier, inc=1, device_id=(p, s), device_id_type=MESH)

    across = space + 2 * core - 1
    has_across = jnp.logical_and(across >= 0, across < 2 * chips)
    expected = half_poles + has_across.astype(jnp.int32) + late.astype(jnp.int32)
    for step in steps:
        expected = expected + has(step).astype(jnp.int32)

        @pl.when(has(step))
        def _():
            greet(pole, space + 2 * step)

    greet(pole, sibling)

    @pl.when(has_across)
    def _():
        greet(pole, across)

    for d in range(1, half_poles):
        greet(half * half_poles + lax.rem(yy + d, half_poles), space)

    @pl.when(early)
    def _():
        greet(partner, space)

    for step in steps:
        @pl.when(jnp.logical_not(has(step)))
        def _():
            zeros = jnp.zeros((4, 8, 8, NZ), jnp.float32)
            kap[pl.ds(HALO + 4 * step, 4)] = zeros
            res[pl.ds(HALO + 4 * step, 4)] = zeros

    @pl.when(jnp.logical_not(has_previous))
    def _():
        fwd[:, 0] = jnp.zeros((4, 8, 8, NZ), jnp.float32)

    @pl.when(jnp.logical_not(has_following))
    def _():
        fwd[:, 3] = jnp.zeros((4, 8, 8, NZ), jnp.float32)

    stage_far[:, :, TOP:] = jnp.zeros((2, 2, NY - TOP, NZ), jnp.float32)
    lane_in = lax.rem(lax.broadcasted_iota(jnp.int32, (3 * NZ, 2 * NZ), 0), NZ)
    lane_out = lax.broadcasted_iota(jnp.int32, (3 * NZ, 2 * NZ), 1)
    source_lane = jnp.where(lane_out < NZ, lane_out + 1, lane_out - NZ - 1)
    shifts[...] = jnp.where(lane_in == source_lane, 1.0, 0.0).astype(jnp.bfloat16)

    for copy in own_copies:
        copy.wait()
    for n in range(2):
        kap[own + n] = 0.5 * natural(stage, (0, n))
        res[own + n] = natural(stage, (1, n))
        for slot in range(2):
            fwd[slot, 1 + n] = natural(stage, (2 + slot, n))
    pole_here = order_mem[core]
    own_shift = shift_mem[pole_here]
    param[0, 0] = jnp.full((8, NZ), own_shift, jnp.float32)
    param[0, 1] = jnp.full((8, NZ), weight_mem[pole_here], jnp.float32)

    pl.semaphore_wait(barrier, expected)

    def send_token(k):
        for a, step in enumerate((TOKENS[k], -TOKENS[k])):
            @pl.when(has(step))
            def _():
                pl.semaphore_signal(token.at[k, a], inc=1, device_id=(pole, space + 2 * step), device_id_type=MESH)

    def take_token(k):
        for a, step in enumerate((TOKENS[k], -TOKENS[k])):
            @pl.when(has(-step))
            def _():
                pl.semaphore_wait(token.at[k, a], 1)

    send_token(0)

    def remote(src, dst, send, recv, p, s):
        return pltpu.make_async_remote_copy(
            src_ref=src, dst_ref=dst, send_sem=send, recv_sem=recv,
            device_id=(p, s), device_id_type=MESH,
        )

    def block_copy(i, step, target):
        return [
            remote(dest.at[pl.ds(own, 2)], dest.at[pl.ds(own - 4 * step, 2)],
                   near_send.at[a, i], near_recv.at[a, i], pole, target)
            for a, dest in enumerate((kap, res))
        ]

    def outgoing(i, step):
        return block_copy(i, step, space + 2 * step)

    def incoming(i, step):
        return block_copy(i, step, space - 2 * step)

    def passing(i, at):
        return [
            remote(dest.at[pl.ds(at, 2)], dest.at[pl.ds(at, 2)], sib_send.at[a, i], sib_recv.at[a, i],
                   pole, sibling)
            for a, dest in enumerate((kap, res))
        ]

    for i, step in enumerate(steps):
        @pl.when(has(step))
        def _():
            for copy in outgoing(i, step):
                copy.start()

    for copy in passing(6, own):
        copy.start()

    far_copies = [
        remote(param.at[0], param.at[1], far_send.at[0], far_recv.at[0], partner, space),
        remote(stage.at[pl.ds(2, 2), :, pl.ds(0, TOP)], stage_far.at[:, :, pl.ds(0, TOP)],
               far_send.at[1], far_recv.at[1], partner, space),
    ]

    @pl.when(late)
    def _():
        for copy in far_copies:
            copy.start()

    def to_previous(k):
        return remote(fwd.at[pl.ds(2 * k, 2), 1], fwd.at[pl.ds(2 * k, 2), 3],
                      f_send.at[2 * k], f_recv.at[2 * k], pole, space - 1)

    def to_following(k):
        return remote(fwd.at[pl.ds(2 * k, 2), 2], fwd.at[pl.ds(2 * k, 2), 0],
                      f_send.at[2 * k + 1], f_recv.at[2 * k + 1], pole, space + 1)

    def send_forward(k):
        @pl.when(has_previous)
        def _():
            to_previous(k).start()

        @pl.when(has_following)
        def _():
            to_following(k).start()

    def wait_forward(k):
        @pl.when(has_previous)
        def _():
            to_following(k).wait_recv()

        @pl.when(has_following)
        def _():
            to_previous(k).wait_recv()

    def sent_forward(k):
        @pl.when(has_previous)
        def _():
            to_previous(k).wait_send()

        @pl.when(has_following)
        def _():
            to_following(k).wait_send()

    send_forward(0)

    block = (8, 8, NZ)
    row = 8 * lax.broadcasted_iota(jnp.int32, block, 1) + lax.broadcasted_iota(jnp.int32, block, 0)
    col = lax.broadcasted_iota(jnp.int32, block, 2)
    row_first, row_last = row == 0, row == NY - 1
    col_first, col_last = col == 0, col == NZ - 1
    top = row < NY // 2
    col_odd = lax.rem(lax.broadcasted_iota(jnp.int32, (4, 8, NZ), 2), 2) == 1

    def inside(i):
        plane = 4 * chip + i - HALO
        return jnp.logical_and(plane >= 0, plane < 4 * chips)

    def fine_faces(i, odd):
        k = kap[i]
        fx, bx = k + kap[i + 1], k + kap[i - 1]
        py = k + jnp.where(row_last, 0.0, next_row(k))
        qy = jnp.where(row_first, k, previous_row(py))
        pz = k + jnp.where(col_last, 0.0, roll(k, -1, 2))
        qz = jnp.where(col_first, k, roll(pz, 1, 2))
        my, mz = jnp.where(row_last, 0.0, py), jnp.where(col_last, 0.0, pz)
        face_x[i] = fx
        face_y[i] = my
        face_z[i] = mz
        down_z[i] = jnp.where(col_first, 0.0, qz)
        b = (fx + bx) + (py + qy) + (pz + qz)
        base[i] = b
        d = b + own_shift
        g = jnp.where(inside(i), W, 0.0) / d
        diag[i] = d
        gain[i] = g
        z1[i] = g * res[i]
        around = row_pairs(fx if odd else bx), rows_of(qy)[0] + rows_of(py)[1], row_pairs(pz), row_pairs(qz)
        return fx, around, rows_of(my)[1], row_pairs(mz)

    def faces(j):
        i = 2 * j
        _, (bx0, by0, pz0, qz0), fy0, fz0 = fine_faces(i, False)
        fx, (bx1, by1, pz1, qz1), fy1, fz1 = fine_faces(i + 1, True)
        cface_x[j] = pair_sum(fx)
        fy = fy0 + fy1
        cface_y[j] = fy + roll(fy, -1, 2)
        cface_z[j] = roll(fz0 + fz1, -1, 2)
        both = (bx0 + bx1) + (by0 + by1)
        d = both + (qz0 + qz1) + roll(both + (pz0 + pz1), -1, 2)
        cbase[j] = d
        cgain[j] = jnp.where(inside(i), W, 0.0) / (d + 8.0 * own_shift)

    middle = HALO // 2
    other = HALO + 2 * (1 - core)
    for copy in passing(6, other):
        copy.wait_recv()
    for ring in range(3):
        pair = tuple(enumerate(steps))[2 * ring : 2 * ring + 2]
        for i, step in pair:
            @pl.when(has(-step))
            def _():
                for copy in incoming(i, step):
                    copy.wait_recv()
                for copy in passing(i, own - 4 * step):
                    copy.start()
        for i, step in pair:
            @pl.when(has(-step))
            def _():
                for copy in passing(i, other - 4 * step):
                    copy.wait_recv()
        take_token(ring)
        send_token(ring + 1)
        if ring == 0:
            rows = (middle - 1, middle, middle + 1, middle + 2)
        else:
            rows = (middle - 2 * ring - 1, middle - 2 * ring, middle + 2 * ring + 1, middle + 2 * ring + 2)
        for j in rows:
            faces(j)
    face_x[0] = kap[0] + kap[1]
    fine_faces(1, True)
    fine_faces(PLANES - 2, False)

    def off(vm, v, vp, fm, fx, fy):
        total = fx * vp + fm * vm
        return total + (fy * next_row(v) + previous_row(fy * v))

    def lane_rolls(fz, v, by):
        return fz * roll(v, -by, 2) + roll(fz * v, by, 2)

    def fine_lanes(i, v):
        if i % 2:
            return lane_rolls(face_z[i], v, 1)
        after, before = lane_sides(v, shifts[...])
        return face_z[i] * after + down_z[i] * before

    def coarse_lanes(j, v):
        return lane_rolls(cface_z[j], v, 2)

    def sweep(ref, lo, hi, faces_xy, lanes, emit):
        px, py = faces_xy
        vm, v, fm = ref[lo - 1], ref[lo], px[lo - 1]
        for i in range(lo, hi):
            vp, fx = ref[i + 1], px[i]
            emit(i, off(vm, v, vp, fm, fx, py[i]) + lanes(i, v), v)
            vm, v, fm = v, vp, fx

    fine_xy, coarse_xy = (face_x, face_y), (cface_x, cface_y)

    def precondition(source, out, lo, hi):
        first, last = (lo - 1) // 2, hi // 2
        held = []

        def down(i, part_off, v):
            held.append(0.2 * source[i] + part_off)
            if i % 2:
                y1[i // 2] = cgain[i // 2] * pair_sum(held[-2] + held[-1])

        def up(j, part_off, v):
            i = 2 * j
            y2 = 1.2 * v + cgain[j] * part_off
            y2 = jnp.where(col_odd, roll(y2, 1, 2), y2)
            y2 = jnp.stack([y2, y2], axis=1).reshape(block)
            z2[i] = z1[i] + y2
            z2[i + 1] = z1[i + 1] + y2

        def smooth(i, part_off, v):
            out[i] = 0.2 * v + z1[i] + gain[i] * part_off

        sweep(z1, 2 * first - 2, 2 * last + 4, fine_xy, fine_lanes, down)
        sweep(y1, first, last + 1, coarse_xy, coarse_lanes, up)
        sweep(z2, lo, hi, fine_xy, fine_lanes, smooth)

    window = HALO - 1 + 2 * core
    sib_window = HALO + 1 - 2 * core

    def exchange(e):
        return [
            remote(mine.at[e, pl.ds(sib_window, 4)], theirs.at[e], xs_send.at[e, a], xs_recv.at[e, a],
                   pole, sibling)
            for a, (mine, theirs) in enumerate(((u0, sib_u), (ut, sib_t)))
        ]

    sub = lax.broadcasted_iota(jnp.int32, (8, NZ), 0)
    lane = lax.broadcasted_iota(jnp.int32, (8, NZ), 1)
    part[0] = jnp.zeros((8, NZ), jnp.float32)

    def solve(e, carry):
        @pl.when(e == 1)
        def _():
            far_copies[0].wait_recv()
            shift = param[1, 0]
            for i in range(1, PLANES - 1):
                d = base[i] + shift
                g = jnp.where(inside(i), W, 0.0) / d
                diag[i] = d
                gain[i] = g
                z1[i] = g * res[i]
            for j in range(1, PLANES // 2 - 1):
                cgain[j] = jnp.where(inside(2 * j), W, 0.0) / (cbase[j] + 8.0 * shift)

        u, t = u0.at[e], ut.at[e]
        precondition(res, u, HALO - 6, HALO + 10)

        def residual(i, part_off, v):
            value = res[i] - (diag[i] * v - part_off)
            rt[i] = value
            z1[i] = gain[i] * value

        sweep(u, HALO - 5, HALO + 9, fine_xy, fine_lanes, residual)
        precondition(rt, t, HALO - 1, HALO + 5)
        for copy in exchange(e):
            copy.start()
        totals = [jnp.zeros((8, NZ), jnp.float32)] * 4

        def products(i, part_off, v):
            image = diag[i] * v - part_off
            un, rn, tn = u[i], res[i], rt[i]
            for k, product in enumerate((un * rn, un * tn, tn * v, v * image)):
                totals[k] = totals[k] + jnp.sum(product, axis=0)

        sweep(t, HALO, HALO + 4, fine_xy, fine_lanes, products)
        tile = part[0]
        for k, total in enumerate(totals):
            tile = jnp.where(sub == 4 * e + k, jnp.sum(total, axis=0, keepdims=True), tile)
        part[0] = tile
        return carry

    lax.fori_loop(0, 2 - half, solve, 0)
    take_token(len(TOKENS) - 1)

    def reduce_start(d, carry):
        remote(part.at[0], part.at[d], ar_send, ar_recv, pole, lax.rem(space + 2 * d, 2 * chips)).start()
        return carry

    lax.fori_loop(1, chips, reduce_start, 0)

    @pl.when(early)
    def _():
        far_copies[1].wait_recv()
        for slot in range(2):
            for n in range(2):
                fwd[2 + slot, 1 + n] = natural(stage_far, (slot, n))
        send_forward(1)

    def everyone(sem):
        return pltpu.make_async_copy(part.at[pl.ds(1, chips - 1)], part.at[pl.ds(1, chips - 1)], sem)

    everyone(ar_recv).wait()
    total = jnp.sum(jnp.sum(part[...], axis=0), axis=1, keepdims=True)
    factors = []
    for e in range(2):
        g0, d0, e1, m0 = (total[4 * e + k : 4 * e + k + 1] for k in range(4))
        weight = param[e, 1][0:1, 0:1]
        c0 = g0 - d0
        eta = d0 / c0
        a0 = 1.0 + eta
        t = d0 - e1
        k = c0 - t
        g1 = e1 - 2.0 * eta * t + eta * eta * k
        b = g1 / g0
        s11 = m0 - 2.0 * eta * (t - m0) + eta * eta * (k - t + m0)
        c1 = s11 + 2.0 * b * (t - eta * k) + b * b * c0
        a1 = g1 / c1
        factors += [weight * (a0 + a1 * (b - eta)), weight * (a1 * a0)]
    tile = jnp.broadcast_to(factors[0], (8, NZ))
    for k in range(1, 4):
        tile = jnp.where(lane == k, factors[k], tile)
    sums[...] = tile
    scalars = remote(sums, swap, sw_send, sw_recv, pole, sibling)
    scalars.start()

    def combine(source_u, source_t, at, slot, one, two):
        for n in range(4):
            xout[slot, n] = one * source_u[at + n] + two * source_t[at + n]

    combine(u0.at[0], ut.at[0], window, core, factors[0], factors[1])

    @pl.when(early)
    def _():
        combine(u0.at[1], ut.at[1], window, 2 + core, sums[0:1, 2:3], sums[0:1, 3:4])

    for copy in exchange(0):
        copy.wait_recv()
    scalars.wait_recv()
    combine(sib_u.at[0], sib_t.at[0], 0, 1 - core, swap[0:1, 0:1], swap[0:1, 1:2])

    @pl.when(early)
    def _():
        for copy in exchange(1):
            copy.wait_recv()
        combine(sib_u.at[1], sib_t.at[1], 0, 3 - core, swap[0:1, 2:3], swap[0:1, 3:4])
        wait_forward(1)

    wait_forward(0)

    def ahead_row(v):
        return jnp.where(row_last, 0.0, next_row(v))

    def ahead_col(v):
        return jnp.where(col_last, 0.0, roll(v, -1, 2))

    def slot_term(slot, n):
        x, f = xout[slot, n], fwd[slot, n]
        total = (x - xout[slot, n + 1]) * (f - fwd[slot, n + 1])
        total = total + (x - xout[slot, n - 1]) * (f - fwd[slot, n - 1])
        product = x * f
        ahead = (x - ahead_row(x)) * (f - ahead_row(f))
        total = total + ahead + jnp.where(row_first, product, previous_row(ahead))
        ahead = (x - ahead_col(x)) * (f - ahead_col(f))
        return total + ahead + jnp.where(col_first, product, roll(ahead, 1, 2))

    for n in (1, 2):
        mine = slot_term(0, n) + slot_term(1, n)
        extra = lax.fori_loop(
            2, 4 - 2 * half, lambda slot, acc: acc + slot_term(slot, n), jnp.zeros(block, jnp.float32)
        )
        put_natural(term, (n - 1,), -0.5 * (mine + jnp.where(top, extra, 0.0)))

    def rows_for(q):
        return pl.ds(pl.multiple_of(8 * q, 8), 8)

    def spread(d, upper):
        q = lax.rem(yy + d, half_poles)
        k = 0 if upper else 1
        return remote(term.at[:, rows_for(q if upper else q + half_poles), :], pieces.at[k, d],
                      rs_send.at[k, d], rs_recv.at[k, d], half * half_poles + q, space)

    @pl.when(early)
    def _():
        for d in range(1, half_poles):
            spread(d, True).start()

    for d in range(1, half_poles):
        spread(d, False).start()

    for slot in range(2):
        for n in range(2):
            put_natural(xnat, (slot, n), xout[slot, 1 + n])
    adjoint_out = pltpu.make_async_copy(xnat, adjoint_ref, loc.at[0])
    adjoint_out.start()

    share = remote(gfar, gnear, far_send.at[2], far_recv.at[2], partner, space)
    gradient_out = pltpu.make_async_copy(gout, gradient_ref, loc.at[1])

    def collect(k, q):
        total = term[:, rows_for(q), :]
        for d in range(1, half_poles):
            spread(d, k == 0).wait_recv()
            total = total + pieces[k, d]
        return total

    @pl.when(early)
    def _():
        gout[...] = collect(0, yy)
        gradient_out.start()
        gfar[...] = collect(1, yy + half_poles)
        share.start()

    @pl.when(late)
    def _():
        total = collect(1, yy + half_poles)
        share.wait_recv()
        gout[...] = total + gnear[...]
        gradient_out.start()

    for i, step in enumerate(steps):
        @pl.when(has(step))
        def _():
            for copy in outgoing(i, step):
                copy.wait_send()

        @pl.when(has(-step))
        def _():
            for copy in passing(i, own - 4 * step):
                copy.wait_send()
    for copy in passing(6, own):
        copy.wait_send()
    sent_forward(0)
    for copy in exchange(0):
        copy.wait_send()
    everyone(ar_send).wait()
    scalars.wait_send()
    for d in range(1, half_poles):
        spread(d, False).wait_send()

    @pl.when(early)
    def _():
        sent_forward(1)
        for copy in exchange(1):
            copy.wait_send()
        for d in range(1, half_poles):
            spread(d, True).wait_send()
        share.wait_send()

    @pl.when(late)
    def _():
        for copy in far_copies:
            copy.wait_send()

    adjoint_out.wait()
    gradient_out.wait()


def solution(mesh):
    chips, poles = mesh.shape["space"] // 2, mesh.shape["pole"]
    f32 = jnp.float32

    def per_device(conductivity, misfit, forward_states, pole_shifts, pole_weights, pole_order):
        hbm = pl.BlockSpec(memory_space=pltpu.HBM)
        fine = pltpu.VMEM((PLANES, 8, 8, NZ), f32)
        coarse = pltpu.VMEM((PLANES // 2, 4, 8, NZ), f32)
        pair = pltpu.VMEM((2, PLANES, 8, 8, NZ), f32)
        windows = pltpu.VMEM((2, 4, 8, 8, NZ), f32)
        slots = pltpu.VMEM((4, 4, 8, 8, NZ), f32)
        tile = pltpu.VMEM((8, NZ), f32)
        piece = (2, NY // poles, NZ)
        dma = pltpu.SemaphoreType.DMA
        return pl.pallas_call(
            functools.partial(kernel, chips, poles),
            out_shape=(
                jax.ShapeDtypeStruct(forward_states.shape, f32),
                jax.ShapeDtypeStruct(piece, f32),
            ),
            in_specs=[hbm] * 6,
            out_specs=(hbm, hbm),
            scratch_shapes=[
                pltpu.SMEM(pole_shifts.shape, f32), pltpu.SMEM(pole_weights.shape, f32),
                pltpu.SMEM(pole_order.shape, jnp.int32),
            ] + [fine] * 12 + [coarse] * 6 + [
                pair, pair, windows, windows, slots, slots,
                pltpu.VMEM((4, 2, NY, NZ), f32), pltpu.VMEM((2, 2, NY, NZ), f32), pltpu.VMEM((2, 2, NY, NZ), f32),
                pltpu.VMEM((2, NY, NZ), f32), pltpu.VMEM((2, 2, 8, NZ), f32),
                pltpu.VMEM((chips, 8, NZ), f32), tile, tile,
                pltpu.VMEM((2, poles // 2, *piece), f32), pltpu.VMEM(piece, f32), pltpu.VMEM(piece, f32),
                pltpu.VMEM(piece, f32), pltpu.VMEM((3 * NZ, 2 * NZ), jnp.bfloat16),
                dma((6,)), dma((2, 6)), dma((2, 6)), dma((2, 7)), dma((2, 7)), dma((4,)), dma((4,)),
                dma, dma, dma, dma, dma((2, 2)), dma((2, 2)),
                dma((2, poles // 2)), dma((2, poles // 2)), dma((3,)), dma((3,)),
                pltpu.SemaphoreType.REGULAR((len(TOKENS), 2)),
            ],
            compiler_params=pltpu.CompilerParams(
                collective_id=0, has_side_effects=True, vmem_limit_bytes=64 << 20
            ),
            name="adjoint_gradient",
        )(pole_shifts, pole_weights, pole_order, conductivity, misfit, forward_states)

    in_specs = (
        P("space", None, None), P("space", None, None), P("pole", "space", None, None),
        P(), P(), P("pole"),
    )
    out_specs = (P("pole", "space", None, None), P("space", "pole", None))
    return jax.shard_map(per_device, mesh=mesh, in_specs=in_specs, out_specs=out_specs, check_vma=False)
```

```python
import functools

import jax
import jax.numpy as jnp
from jax import lax
from jax.experimental import pallas as pl
from jax.experimental.pallas import tpu as pltpu
from jax.sharding import PartitionSpec as P

MESH = pl.DeviceIdType.MESH
W = 0.8
NY, NZ = 64, 128
HALO = 12
PLANES = 4 + 2 * HALO
TOKENS = (3, 6, 12, 24)
TOP = NY // 2 + 8


def roll(value, shift, axis):
    return pltpu.roll(value, shift % value.shape[axis], axis)


def next_row(value):
    return jnp.concatenate([value[1:], roll(value[:1], -1, 1)], axis=0)


def previous_row(value):
    return jnp.concatenate([roll(value[-1:], 1, 1), value[:-1]], axis=0)


def rows_of(value):
    pairs = value.reshape(value.shape[0] // 2, 2, *value.shape[1:])
    return pairs[:, 0], pairs[:, 1]


def row_pairs(value):
    even, odd = rows_of(value)
    return even + odd


def pair_sum(value):
    value = row_pairs(value)
    return value + roll(value, -1, 2)


def lane_sides(value, shifts):
    rows = value.reshape(-1, NZ)
    high = rows.astype(jnp.bfloat16)
    rest = rows - high.astype(jnp.float32)
    mid = rest.astype(jnp.bfloat16)
    low = (rest - mid.astype(jnp.float32)).astype(jnp.bfloat16)
    out = jnp.dot(jnp.concatenate([high, mid, low], axis=1), shifts, preferred_element_type=jnp.float32)
    return out[:, :NZ].reshape(value.shape), out[:, NZ:].reshape(value.shape)


def natural(ref, index):
    return jnp.stack([ref[(*index, pl.ds(v, 8, stride=8), slice(None))] for v in range(8)])


def put_natural(ref, index, value):
    for v in range(8):
        ref[(*index, pl.ds(v, 8, stride=8), slice(None))] = value[v]


def kernel(
    chips, poles,
    shift_ref, weight_ref, order_ref, kappa_ref, misfit_ref, forward_ref,
    adjoint_ref, gradient_ref,
    shift_mem, weight_mem, order_mem,
    kap, res, face_x, face_y, face_z, down_z, base, diag, gain, z1, z2, rt,
    cface_x, cface_y, cface_z, cbase, cgain, y1, u0, ut,
    sib_u, sib_t, fwd, parts, stage, stage_far, xnat, term, param, part, sums, swap, pieces, gout, gfar, gnear, shifts,
    loc, near_send, near_recv, sib_send, sib_recv, f_send, f_recv, ar_send, ar_recv, sw_send, sw_recv,
    xs_send, xs_recv, rs_send, rs_recv, far_send, far_recv, y_send, y_recv, token,
):
    half_poles = poles // 2
    pole = lax.axis_index("pole")
    space = lax.axis_index("space")
    half, yy = pole // half_poles, lax.rem(pole, half_poles)
    early, late = half == 0, half == 1
    partner = lax.rem(pole + half_poles, poles)
    core = lax.rem(space, 2)
    chip = space // 2
    sibling = space + 1 - 2 * core
    has_previous, has_following = space > 0, space < 2 * chips - 1
    steps = (1, -1, 2, -2, 3, -3)

    def has(step):
        return jnp.logical_and(chip + step >= 0, chip + step < chips)

    own = HALO + 2 * core
    own_copies = [
        pltpu.make_async_copy(kappa_ref, stage.at[0], loc.at[0]),
        pltpu.make_async_copy(misfit_ref, stage.at[1], loc.at[1]),
        pltpu.make_async_copy(forward_ref, stage.at[pl.ds(2, 2)], loc.at[2]),
        pltpu.make_async_copy(shift_ref, shift_mem, loc.at[3]),
        pltpu.make_async_copy(weight_ref, weight_mem, loc.at[4]),
        pltpu.make_async_copy(order_ref, order_mem, loc.at[5]),
    ]
    for copy in own_copies:
        copy.start()

    barrier = pltpu.get_barrier_semaphore()

    def greet(p, s):
        pl.semaphore_signal(barrier, inc=1, device_id=(p, s), device_id_type=MESH)

    across = space + 2 * core - 1
    has_across = jnp.logical_and(across >= 0, across < 2 * chips)
    expected = half_poles + has_across.astype(jnp.int32) + late.astype(jnp.int32)
    for step in steps:
        expected = expected + has(step).astype(jnp.int32)

        @pl.when(has(step))
        def _():
            greet(pole, space + 2 * step)

    greet(pole, sibling)

    @pl.when(has_across)
    def _():
        greet(pole, across)

    for d in range(1, half_poles):
        greet(half * half_poles + lax.rem(yy + d, half_poles), space)

    @pl.when(early)
    def _():
        greet(partner, space)

    for step in steps:
        @pl.when(jnp.logical_not(has(step)))
        def _():
            zeros = jnp.zeros((4, 8, 8, NZ), jnp.float32)
            kap[pl.ds(HALO + 4 * step, 4)] = zeros
            res[pl.ds(HALO + 4 * step, 4)] = zeros

    @pl.when(jnp.logical_not(has_previous))
    def _():
        fwd[:, 0] = jnp.zeros((4, 8, 8, NZ), jnp.float32)

    @pl.when(jnp.logical_not(has_following))
    def _():
        fwd[:, 3] = jnp.zeros((4, 8, 8, NZ), jnp.float32)

    stage_far[:, :, TOP:] = jnp.zeros((2, 2, NY - TOP, NZ), jnp.float32)
    lane_in = lax.rem(lax.broadcasted_iota(jnp.int32, (3 * NZ, 2 * NZ), 0), NZ)
    lane_out = lax.broadcasted_iota(jnp.int32, (3 * NZ, 2 * NZ), 1)
    source_lane = jnp.where(lane_out < NZ, lane_out + 1, lane_out - NZ - 1)
    shifts[...] = jnp.where(lane_in == source_lane, 1.0, 0.0).astype(jnp.bfloat16)

    for copy in own_copies:
        copy.wait()
    for n in range(2):
        kap[own + n] = 0.5 * natural(stage, (0, n))
        res[own + n] = natural(stage, (1, n))
        for slot in range(2):
            fwd[slot, 1 + n] = natural(stage, (2 + slot, n))
    pole_here = order_mem[core]
    own_shift = shift_mem[pole_here]
    param[0, 0] = jnp.full((8, NZ), own_shift, jnp.float32)
    param[0, 1] = jnp.full((8, NZ), weight_mem[pole_here], jnp.float32)

    pl.semaphore_wait(barrier, expected)

    def send_token(k):
        for a, step in enumerate((TOKENS[k], -TOKENS[k])):
            @pl.when(has(step))
            def _():
                pl.semaphore_signal(token.at[k, a], inc=1, device_id=(pole, space + 2 * step), device_id_type=MESH)

    def take_token(k):
        for a, step in enumerate((TOKENS[k], -TOKENS[k])):
            @pl.when(has(-step))
            def _():
                pl.semaphore_wait(token.at[k, a], 1)

    send_token(0)

    def remote(src, dst, send, recv, p, s):
        return pltpu.make_async_remote_copy(
            src_ref=src, dst_ref=dst, send_sem=send, recv_sem=recv,
            device_id=(p, s), device_id_type=MESH,
        )

    part_rows = 8 // half_poles
    my_part = pl.ds(part_rows * yy, part_rows)

    def block_copy(i, step, target):
        share = (my_part,) if abs(step) >= 2 else ()
        return [
            remote(dest.at[(pl.ds(own, 2), *share)], dest.at[(pl.ds(own - 4 * step, 2), *share)],
                   near_send.at[a, i], near_recv.at[a, i], pole, target)
            for a, dest in enumerate((kap, res))
        ]

    def share_copy(i, step):
        at = (pl.ds(own - 4 * step, 2), my_part)
        return [
            remote(dest.at[at], dest.at[at], y_send.at[a, i - 2, d], y_recv.at[a, i - 2, d],
                   half * half_poles + lax.rem(yy + d, half_poles), space)
            for a, dest in enumerate((kap, res)) for d in range(1, half_poles)
        ]

    def outgoing(i, step):
        return block_copy(i, step, space + 2 * step)

    def incoming(i, step):
        return block_copy(i, step, space - 2 * step)

    def passing(i, at):
        return [
            remote(dest.at[pl.ds(at, 2)], dest.at[pl.ds(at, 2)], sib_send.at[a, i], sib_recv.at[a, i],
                   pole, sibling)
            for a, dest in enumerate((kap, res))
        ]

    for i in (2, 3, 4, 5, 0, 1):
        @pl.when(has(steps[i]))
        def _():
            for copy in outgoing(i, steps[i]):
                copy.start()

    for copy in passing(6, own):
        copy.start()

    far_copies = [
        remote(param.at[0], param.at[1], far_send.at[0], far_recv.at[0], partner, space),
        remote(stage.at[pl.ds(2, 2), :, pl.ds(0, TOP)], stage_far.at[:, :, pl.ds(0, TOP)],
               far_send.at[1], far_recv.at[1], partner, space),
    ]

    @pl.when(late)
    def _():
        for copy in far_copies:
            copy.start()

    def to_previous(k):
        return remote(fwd.at[pl.ds(2 * k, 2), 1], fwd.at[pl.ds(2 * k, 2), 3],
                      f_send.at[2 * k], f_recv.at[2 * k], pole, space - 1)

    def to_following(k):
        return remote(fwd.at[pl.ds(2 * k, 2), 2], fwd.at[pl.ds(2 * k, 2), 0],
                      f_send.at[2 * k + 1], f_recv.at[2 * k + 1], pole, space + 1)

    def send_forward(k):
        @pl.when(has_previous)
        def _():
            to_previous(k).start()

        @pl.when(has_following)
        def _():
            to_following(k).start()

    def wait_forward(k):
        @pl.when(has_previous)
        def _():
            to_following(k).wait_recv()

        @pl.when(has_following)
        def _():
            to_previous(k).wait_recv()

    def sent_forward(k):
        @pl.when(has_previous)
        def _():
            to_previous(k).wait_send()

        @pl.when(has_following)
        def _():
            to_following(k).wait_send()

    send_forward(0)

    block = (8, 8, NZ)
    row = 8 * lax.broadcasted_iota(jnp.int32, block, 1) + lax.broadcasted_iota(jnp.int32, block, 0)
    col = lax.broadcasted_iota(jnp.int32, block, 2)
    row_first, row_last = row == 0, row == NY - 1
    col_first, col_last = col == 0, col == NZ - 1
    top = row < NY // 2
    col_odd = lax.rem(lax.broadcasted_iota(jnp.int32, (4, 8, NZ), 2), 2) == 1

    def inside(i):
        plane = 4 * chip + i - HALO
        return jnp.logical_and(plane >= 0, plane < 4 * chips)

    def fine_faces(i, odd):
        k = kap[i]
        fx, bx = k + kap[i + 1], k + kap[i - 1]
        py = k + jnp.where(row_last, 0.0, next_row(k))
        qy = jnp.where(row_first, k, previous_row(py))
        pz = k + jnp.where(col_last, 0.0, roll(k, -1, 2))
        qz = jnp.where(col_first, k, roll(pz, 1, 2))
        my, mz = jnp.where(row_last, 0.0, py), jnp.where(col_last, 0.0, pz)
        face_x[i] = fx
        face_y[i] = my
        face_z[i] = mz
        down_z[i] = jnp.where(col_first, 0.0, qz)
        b = (fx + bx) + (py + qy) + (pz + qz)
        base[i] = b
        d = b + own_shift
        g = jnp.where(inside(i), W, 0.0) / d
        diag[i] = d
        gain[i] = g
        z1[i] = g * res[i]
        around = row_pairs(fx if odd else bx), rows_of(qy)[0] + rows_of(py)[1], row_pairs(pz), row_pairs(qz)
        return fx, around, rows_of(my)[1], row_pairs(mz)

    def faces(j):
        i = 2 * j
        _, (bx0, by0, pz0, qz0), fy0, fz0 = fine_faces(i, False)
        fx, (bx1, by1, pz1, qz1), fy1, fz1 = fine_faces(i + 1, True)
        cface_x[j] = pair_sum(fx)
        fy = fy0 + fy1
        cface_y[j] = fy + roll(fy, -1, 2)
        cface_z[j] = roll(fz0 + fz1, -1, 2)
        both = (bx0 + bx1) + (by0 + by1)
        d = both + (qz0 + qz1) + roll(both + (pz0 + pz1), -1, 2)
        cbase[j] = d
        cgain[j] = jnp.where(inside(i), W, 0.0) / (d + 8.0 * own_shift)

    middle = HALO // 2
    other = HALO + 2 * (1 - core)
    for copy in passing(6, other):
        copy.wait_recv()
    for i in (2, 3, 4, 5):
        @pl.when(has(-steps[i]))
        def _():
            for copy in incoming(i, steps[i]):
                copy.wait_recv()
            for copy in share_copy(i, steps[i]):
                copy.start()
    for ring in range(3):
        pair = tuple(enumerate(steps))[2 * ring : 2 * ring + 2]
        for i, step in pair:
            @pl.when(has(-step))
            def _():
                for copy in share_copy(i, step) if ring else incoming(i, step):
                    copy.wait_recv()
                for copy in passing(i, own - 4 * step):
                    copy.start()
        for i, step in pair:
            @pl.when(has(-step))
            def _():
                for copy in passing(i, other - 4 * step):
                    copy.wait_recv()
        take_token(ring)
        send_token(ring + 1)
        if ring == 0:
            rows = (middle - 1, middle, middle + 1, middle + 2)
        else:
            rows = (middle - 2 * ring - 1, middle - 2 * ring, middle + 2 * ring + 1, middle + 2 * ring + 2)
        for j in rows:
            faces(j)
    face_x[0] = kap[0] + kap[1]
    fine_faces(1, True)
    fine_faces(PLANES - 2, False)

    def off(vm, v, vp, fm, fx, fy):
        total = fx * vp + fm * vm
        return total + (fy * next_row(v) + previous_row(fy * v))

    def lane_rolls(fz, v, by):
        return fz * roll(v, -by, 2) + roll(fz * v, by, 2)

    def fine_lanes(i, v):
        if i % 2:
            return lane_rolls(face_z[i], v, 1)
        after, before = lane_sides(v, shifts[...])
        return face_z[i] * after + down_z[i] * before

    def coarse_lanes(j, v):
        return lane_rolls(cface_z[j], v, 2)

    def sweep(ref, lo, hi, faces_xy, lanes, emit):
        px, py = faces_xy
        vm, v, fm = ref[lo - 1], ref[lo], px[lo - 1]
        for i in range(lo, hi):
            vp, fx = ref[i + 1], px[i]
            emit(i, off(vm, v, vp, fm, fx, py[i]) + lanes(i, v), v)
            vm, v, fm = v, vp, fx

    fine_xy, coarse_xy = (face_x, face_y), (cface_x, cface_y)

    def precondition(source, out, lo, hi):
        first, last = (lo - 1) // 2, hi // 2
        held = []

        def down(i, part_off, v):
            held.append(0.2 * source[i] + part_off)
            if i % 2:
                y1[i // 2] = cgain[i // 2] * pair_sum(held[-2] + held[-1])

        def up(j, part_off, v):
            i = 2 * j
            y2 = 1.2 * v + cgain[j] * part_off
            y2 = jnp.where(col_odd, roll(y2, 1, 2), y2)
            y2 = jnp.stack([y2, y2], axis=1).reshape(block)
            z2[i] = z1[i] + y2
            z2[i + 1] = z1[i + 1] + y2

        def smooth(i, part_off, v):
            out[i] = 0.2 * v + z1[i] + gain[i] * part_off

        sweep(z1, 2 * first - 2, 2 * last + 4, fine_xy, fine_lanes, down)
        sweep(y1, first, last + 1, coarse_xy, coarse_lanes, up)
        sweep(z2, lo, hi, fine_xy, fine_lanes, smooth)

    window = HALO - 1 + 2 * core
    sib_window = HALO + 1 - 2 * core

    def exchange(e):
        return [
            remote(mine.at[e, pl.ds(sib_window, 4)], theirs.at[e], xs_send.at[e, a], xs_recv.at[e, a],
                   pole, sibling)
            for a, (mine, theirs) in enumerate(((u0, sib_u), (ut, sib_t)))
        ]

    sub = lax.broadcasted_iota(jnp.int32, (8, NZ), 0)
    lane = lax.broadcasted_iota(jnp.int32, (8, NZ), 1)
    part[0] = jnp.zeros((8, NZ), jnp.float32)

    def solve(e, carry):
        @pl.when(e == 1)
        def _():
            far_copies[0].wait_recv()
            shift = param[1, 0]
            for i in range(1, PLANES - 1):
                d = base[i] + shift
                g = jnp.where(inside(i), W, 0.0) / d
                diag[i] = d
                gain[i] = g
                z1[i] = g * res[i]
            for j in range(1, PLANES // 2 - 1):
                cgain[j] = jnp.where(inside(2 * j), W, 0.0) / (cbase[j] + 8.0 * shift)

        u, t = u0.at[e], ut.at[e]
        precondition(res, u, HALO - 6, HALO + 10)

        def residual(i, part_off, v):
            value = res[i] - (diag[i] * v - part_off)
            rt[i] = value
            z1[i] = gain[i] * value

        sweep(u, HALO - 5, HALO + 9, fine_xy, fine_lanes, residual)
        precondition(rt, t, HALO - 1, HALO + 5)
        for copy in exchange(e):
            copy.start()
        totals = [jnp.zeros((8, NZ), jnp.float32)] * 4

        def products(i, part_off, v):
            image = diag[i] * v - part_off
            un, rn, tn = u[i], res[i], rt[i]
            for k, product in enumerate((un * rn, un * tn, tn * v, v * image)):
                totals[k] = totals[k] + jnp.sum(product, axis=0)

        sweep(t, HALO, HALO + 4, fine_xy, fine_lanes, products)
        tile = part[0]
        for k, total in enumerate(totals):
            tile = jnp.where(sub == 4 * e + k, jnp.sum(total, axis=0, keepdims=True), tile)
        part[0] = tile
        return carry

    lax.fori_loop(0, 2 - half, solve, 0)
    take_token(len(TOKENS) - 1)

    def reduce_start(d, carry):
        remote(part.at[0], part.at[d], ar_send, ar_recv, pole, lax.rem(space + 2 * d, 2 * chips)).start()
        return carry

    lax.fori_loop(1, chips, reduce_start, 0)

    def ahead_row(v):
        return jnp.where(row_last, 0.0, next_row(v))

    def ahead_col(v):
        return jnp.where(col_last, 0.0, roll(v, -1, 2))

    def slot_terms(e, who, fields, at):
        slot = 2 * e + (core if who == 0 else 1 - core)
        for n in (1, 2):
            f = fwd[slot, n]
            f_next, f_last = f - fwd[slot, n + 1], f - fwd[slot, n - 1]
            f_row, f_col = f - ahead_row(f), f - ahead_col(f)
            for k, ref in enumerate(fields):
                x = ref[at + n]
                total = (x - ref[at + n + 1]) * f_next + (x - ref[at + n - 1]) * f_last
                product = x * f
                ahead = (x - ahead_row(x)) * f_row
                total = total + ahead + jnp.where(row_first, product, previous_row(ahead))
                ahead = (x - ahead_col(x)) * f_col
                parts[e, who, k, n - 1] = total + ahead + jnp.where(col_first, product, roll(ahead, 1, 2))

    for copy in exchange(0):
        copy.wait_recv()
    wait_forward(0)
    slot_terms(0, 0, (u0.at[0], ut.at[0]), window)
    slot_terms(0, 1, (sib_u.at[0], sib_t.at[0]), 0)

    @pl.when(early)
    def _():
        far_copies[1].wait_recv()
        for slot in range(2):
            for n in range(2):
                fwd[2 + slot, 1 + n] = natural(stage_far, (slot, n))
        send_forward(1)
        for copy in exchange(1):
            copy.wait_recv()
        wait_forward(1)
        slot_terms(1, 0, (u0.at[1], ut.at[1]), window)
        slot_terms(1, 1, (sib_u.at[1], sib_t.at[1]), 0)

    def everyone(sem):
        return pltpu.make_async_copy(part.at[pl.ds(1, chips - 1)], part.at[pl.ds(1, chips - 1)], sem)

    everyone(ar_recv).wait()
    total = jnp.sum(jnp.sum(part[...], axis=0), axis=1, keepdims=True)
    factors = []
    for e in range(2):
        g0, d0, e1, m0 = (total[4 * e + k : 4 * e + k + 1] for k in range(4))
        weight = param[e, 1][0:1, 0:1]
        c0 = g0 - d0
        eta = d0 / c0
        a0 = 1.0 + eta
        t = d0 - e1
        k = c0 - t
        g1 = e1 - 2.0 * eta * t + eta * eta * k
        b = g1 / g0
        s11 = m0 - 2.0 * eta * (t - m0) + eta * eta * (k - t + m0)
        c1 = s11 + 2.0 * b * (t - eta * k) + b * b * c0
        a1 = g1 / c1
        factors += [weight * (a0 + a1 * (b - eta)), weight * (a1 * a0)]
    tile = jnp.broadcast_to(factors[0], (8, NZ))
    for k in range(1, 4):
        tile = jnp.where(lane == k, factors[k], tile)
    sums[...] = tile
    scalars = remote(sums, swap, sw_send, sw_recv, pole, sibling)
    scalars.start()
    scalars.wait_recv()

    def weighted(e, n):
        factor = [ref[0:1, 2 * e + k : 2 * e + k + 1] for ref in (sums, swap) for k in range(2)]
        own_part = factor[0] * parts[e, 0, 0, n] + factor[1] * parts[e, 0, 1, n]
        return own_part + (factor[2] * parts[e, 1, 0, n] + factor[3] * parts[e, 1, 1, n])

    @pl.when(late)
    def _():
        for n in range(2):
            put_natural(term, (n,), -0.5 * weighted(0, n))

    @pl.when(early)
    def _():
        for n in range(2):
            put_natural(term, (n,), -0.5 * (weighted(0, n) + jnp.where(top, weighted(1, n), 0.0)))

    def rows_for(q):
        return pl.ds(pl.multiple_of(8 * q, 8), 8)

    def spread(d, upper):
        q = lax.rem(yy + d, half_poles)
        k = 0 if upper else 1
        return remote(term.at[:, rows_for(q if upper else q + half_poles), :], pieces.at[k, d],
                      rs_send.at[k, d], rs_recv.at[k, d], half * half_poles + q, space)

    @pl.when(early)
    def _():
        for d in range(1, half_poles):
            spread(d, True).start()

    for d in range(1, half_poles):
        spread(d, False).start()

    for ref, fields, at, slot in ((sums, (u0.at[0], ut.at[0]), window, core), (swap, (sib_u.at[0], sib_t.at[0]), 0, 1 - core)):
        for n in range(2):
            value = ref[0:1, 0:1] * fields[0][at + 1 + n] + ref[0:1, 1:2] * fields[1][at + 1 + n]
            put_natural(xnat, (slot, n), value)
    adjoint_out = pltpu.make_async_copy(xnat, adjoint_ref, loc.at[0])
    adjoint_out.start()

    share = remote(gfar, gnear, far_send.at[2], far_recv.at[2], partner, space)
    gradient_out = pltpu.make_async_copy(gout, gradient_ref, loc.at[1])

    def collect(k, q):
        total = term[:, rows_for(q), :]
        for d in range(1, half_poles):
            spread(d, k == 0).wait_recv()
            total = total + pieces[k, d]
        return total

    @pl.when(early)
    def _():
        gout[...] = collect(0, yy)
        gradient_out.start()
        gfar[...] = collect(1, yy + half_poles)
        share.start()

    @pl.when(late)
    def _():
        total = collect(1, yy + half_poles)
        share.wait_recv()
        gout[...] = total + gnear[...]
        gradient_out.start()

    for i, step in enumerate(steps):
        @pl.when(has(step))
        def _():
            for copy in outgoing(i, step):
                copy.wait_send()

        @pl.when(has(-step))
        def _():
            for copy in passing(i, own - 4 * step):
                copy.wait_send()
            if abs(step) >= 2:
                for copy in share_copy(i, step):
                    copy.wait_send()
    for copy in passing(6, own):
        copy.wait_send()
    sent_forward(0)
    for copy in exchange(0):
        copy.wait_send()
    everyone(ar_send).wait()
    scalars.wait_send()
    for d in range(1, half_poles):
        spread(d, False).wait_send()

    @pl.when(early)
    def _():
        sent_forward(1)
        for copy in exchange(1):
            copy.wait_send()
        for d in range(1, half_poles):
            spread(d, True).wait_send()
        share.wait_send()

    @pl.when(late)
    def _():
        for copy in far_copies:
            copy.wait_send()

    adjoint_out.wait()
    gradient_out.wait()


def solution(mesh):
    chips, poles = mesh.shape["space"] // 2, mesh.shape["pole"]
    f32 = jnp.float32

    def per_device(conductivity, misfit, forward_states, pole_shifts, pole_weights, pole_order):
        hbm = pl.BlockSpec(memory_space=pltpu.HBM)
        fine = pltpu.VMEM((PLANES, 8, 8, NZ), f32)
        coarse = pltpu.VMEM((PLANES // 2, 4, 8, NZ), f32)
        pair = pltpu.VMEM((2, PLANES, 8, 8, NZ), f32)
        windows = pltpu.VMEM((2, 4, 8, 8, NZ), f32)
        slots = pltpu.VMEM((4, 4, 8, 8, NZ), f32)
        tile = pltpu.VMEM((8, NZ), f32)
        piece = (2, NY // poles, NZ)
        dma = pltpu.SemaphoreType.DMA
        return pl.pallas_call(
            functools.partial(kernel, chips, poles),
            out_shape=(
                jax.ShapeDtypeStruct(forward_states.shape, f32),
                jax.ShapeDtypeStruct(piece, f32),
            ),
            in_specs=[hbm] * 6,
            out_specs=(hbm, hbm),
            scratch_shapes=[
                pltpu.SMEM(pole_shifts.shape, f32), pltpu.SMEM(pole_weights.shape, f32),
                pltpu.SMEM(pole_order.shape, jnp.int32),
            ] + [fine] * 12 + [coarse] * 6 + [
                pair, pair, windows, windows, slots, pltpu.VMEM((2, 2, 2, 2, 8, 8, NZ), f32),
                pltpu.VMEM((4, 2, NY, NZ), f32), pltpu.VMEM((2, 2, NY, NZ), f32), pltpu.VMEM((2, 2, NY, NZ), f32),
                pltpu.VMEM((2, NY, NZ), f32), pltpu.VMEM((2, 2, 8, NZ), f32),
                pltpu.VMEM((chips, 8, NZ), f32), tile, tile,
                pltpu.VMEM((2, poles // 2, *piece), f32), pltpu.VMEM(piece, f32), pltpu.VMEM(piece, f32),
                pltpu.VMEM(piece, f32), pltpu.VMEM((3 * NZ, 2 * NZ), jnp.bfloat16),
                dma((6,)), dma((2, 6)), dma((2, 6)), dma((2, 7)), dma((2, 7)), dma((4,)), dma((4,)),
                dma, dma, dma, dma, dma((2, 2)), dma((2, 2)),
                dma((2, poles // 2)), dma((2, poles // 2)), dma((3,)), dma((3,)),
                dma((2, 4, poles // 2)), dma((2, 4, poles // 2)), pltpu.SemaphoreType.REGULAR((len(TOKENS), 2)),
            ],
            compiler_params=pltpu.CompilerParams(
                collective_id=0, has_side_effects=True, vmem_limit_bytes=64 << 20
            ),
            name="adjoint_gradient",
        )(pole_shifts, pole_weights, pole_order, conductivity, misfit, forward_states)

    in_specs = (
        P("space", None, None), P("space", None, None), P("pole", "space", None, None),
        P(), P(), P("pole"),
    )
    out_specs = (P("pole", "space", None, None), P("space", "pole", None))
    return jax.shard_map(per_device, mesh=mesh, in_specs=in_specs, out_specs=out_specs, check_vma=False)
```

```python
import functools

import jax
import jax.numpy as jnp
from jax import lax
from jax.experimental import pallas as pl
from jax.experimental.pallas import tpu as pltpu
from jax.sharding import PartitionSpec as P

MESH = pl.DeviceIdType.MESH
W = 0.8
NY, NZ = 64, 128
HALO = 12
PLANES = 4 + 2 * HALO
TOKENS = (3, 6, 12, 24)
TOP = NY // 2 + 8


def roll(value, shift, axis):
    return pltpu.roll(value, shift % value.shape[axis], axis)


def next_row(value):
    return jnp.concatenate([value[1:], roll(value[:1], -1, 1)], axis=0)


def previous_row(value):
    return jnp.concatenate([roll(value[-1:], 1, 1), value[:-1]], axis=0)


def rows_of(value):
    pairs = value.reshape(value.shape[0] // 2, 2, *value.shape[1:])
    return pairs[:, 0], pairs[:, 1]


def row_pairs(value):
    even, odd = rows_of(value)
    return even + odd


def pair_sum(value):
    value = row_pairs(value)
    return value + roll(value, -1, 2)


def lane_sides(value, shifts):
    rows = value.reshape(-1, NZ)
    high = rows.astype(jnp.bfloat16)
    rest = rows - high.astype(jnp.float32)
    mid = rest.astype(jnp.bfloat16)
    low = (rest - mid.astype(jnp.float32)).astype(jnp.bfloat16)
    out = jnp.dot(jnp.concatenate([high, mid, low], axis=1), shifts, preferred_element_type=jnp.float32)
    return out[:, :NZ].reshape(value.shape), out[:, NZ:].reshape(value.shape)


def natural(ref, index):
    return jnp.stack([ref[(*index, pl.ds(v, 8, stride=8), slice(None))] for v in range(8)])


def put_natural(ref, index, value):
    for v in range(8):
        ref[(*index, pl.ds(v, 8, stride=8), slice(None))] = value[v]


def kernel(
    chips, poles,
    shift_ref, weight_ref, order_ref, kappa_ref, misfit_ref, forward_ref,
    adjoint_ref, gradient_ref,
    shift_mem, weight_mem, order_mem,
    both_fields, face_x, face_y, face_z, down_z, base, diag, gain, z1, z2, rt,
    cface_x, cface_y, cface_z, cbase, cgain, y1, u0, ut,
    sib_u, sib_t, fwd, parts, stage, stage_far, term, param, part, sums, swap, pieces, gfar, gnear, shifts,
    loc, near_send, near_recv, sib_send, sib_recv, f_send, f_recv, ar_send, ar_recv, sw_send, sw_recv,
    xs_send, xs_recv, rs_send, rs_recv, far_send, far_recv, y_send, y_recv, token,
):
    half_poles = poles // 2
    kap, res = both_fields.at[0], both_fields.at[1]
    pole = lax.axis_index("pole")
    space = lax.axis_index("space")
    half, yy = pole // half_poles, lax.rem(pole, half_poles)
    early, late = half == 0, half == 1
    partner = lax.rem(pole + half_poles, poles)
    core = lax.rem(space, 2)
    chip = space // 2
    sibling = space + 1 - 2 * core
    has_previous, has_following = space > 0, space < 2 * chips - 1
    steps = (1, -1, 2, -2, 3, -3)

    def has(step):
        return jnp.logical_and(chip + step >= 0, chip + step < chips)

    own = HALO + 2 * core
    own_copies = [
        pltpu.make_async_copy(kappa_ref, stage.at[0], loc.at[0]),
        pltpu.make_async_copy(misfit_ref, stage.at[1], loc.at[1]),
        pltpu.make_async_copy(forward_ref, stage.at[pl.ds(2, 2)], loc.at[2]),
        pltpu.make_async_copy(shift_ref, shift_mem, loc.at[3]),
        pltpu.make_async_copy(weight_ref, weight_mem, loc.at[4]),
        pltpu.make_async_copy(order_ref, order_mem, loc.at[5]),
    ]
    for copy in own_copies:
        copy.start()

    barrier = pltpu.get_barrier_semaphore()

    def greet(p, s):
        pl.semaphore_signal(barrier, inc=1, device_id=(p, s), device_id_type=MESH)

    across = space + 2 * core - 1
    has_across = jnp.logical_and(across >= 0, across < 2 * chips)
    expected = half_poles + has_across.astype(jnp.int32) + late.astype(jnp.int32)
    for step in steps:
        expected = expected + has(step).astype(jnp.int32)

        @pl.when(has(step))
        def _():
            greet(pole, space + 2 * step)

    greet(pole, sibling)

    @pl.when(has_across)
    def _():
        greet(pole, across)

    for d in range(1, half_poles):
        greet(half * half_poles + lax.rem(yy + d, half_poles), space)

    @pl.when(early)
    def _():
        greet(partner, space)

    for step in steps:
        @pl.when(jnp.logical_not(has(step)))
        def _():
            zeros = jnp.zeros((4, 8, 8, NZ), jnp.float32)
            kap[pl.ds(HALO + 4 * step, 4)] = zeros
            res[pl.ds(HALO + 4 * step, 4)] = zeros

    @pl.when(jnp.logical_not(has_previous))
    def _():
        fwd[:, 0] = jnp.zeros((4, 8, 8, NZ), jnp.float32)

    @pl.when(jnp.logical_not(has_following))
    def _():
        fwd[:, 3] = jnp.zeros((4, 8, 8, NZ), jnp.float32)

    stage_far[:, :, TOP:] = jnp.zeros((2, 2, NY - TOP, NZ), jnp.float32)
    lane_in = lax.rem(lax.broadcasted_iota(jnp.int32, (3 * NZ, 2 * NZ), 0), NZ)
    lane_out = lax.broadcasted_iota(jnp.int32, (3 * NZ, 2 * NZ), 1)
    source_lane = jnp.where(lane_out < NZ, lane_out + 1, lane_out - NZ - 1)
    shifts[...] = jnp.where(lane_in == source_lane, 1.0, 0.0).astype(jnp.bfloat16)

    for copy in own_copies:
        copy.wait()
    for n in range(2):
        kap[own + n] = 0.5 * natural(stage, (0, n))
        res[own + n] = natural(stage, (1, n))
        for slot in range(2):
            fwd[slot, 1 + n] = natural(stage, (2 + slot, n))
    pole_here = order_mem[core]
    own_shift = shift_mem[pole_here]
    param[0, 0] = jnp.full((8, NZ), own_shift, jnp.float32)
    param[0, 1] = jnp.full((8, NZ), weight_mem[pole_here], jnp.float32)

    pl.semaphore_wait(barrier, expected)

    def send_token(k):
        for a, step in enumerate((TOKENS[k], -TOKENS[k])):
            @pl.when(has(step))
            def _():
                pl.semaphore_signal(token.at[k, a], inc=1, device_id=(pole, space + 2 * step), device_id_type=MESH)

    def take_token(k):
        for a, step in enumerate((TOKENS[k], -TOKENS[k])):
            @pl.when(has(-step))
            def _():
                pl.semaphore_wait(token.at[k, a], 1)

    send_token(0)

    def remote(src, dst, send, recv, p, s):
        return pltpu.make_async_remote_copy(
            src_ref=src, dst_ref=dst, send_sem=send, recv_sem=recv,
            device_id=(p, s), device_id_type=MESH,
        )

    part_rows = 8 // half_poles
    my_part = pl.ds(part_rows * yy, part_rows)

    def block_copy(i, step, target):
        share = (my_part,) if abs(step) >= 2 else ()
        return [
            remote(both_fields.at[(slice(None), pl.ds(own, 2), *share)],
                   both_fields.at[(slice(None), pl.ds(own - 4 * step, 2), *share)],
                   near_send.at[i], near_recv.at[i], pole, target)
        ]

    def share_copy(i, step):
        block = both_fields.at[:, pl.ds(own - 4 * step, 2), my_part]
        return [
            remote(block, block, y_send.at[i - 2, d], y_recv.at[i - 2, d],
                   half * half_poles + lax.rem(yy + d, half_poles), space)
            for d in range(1, half_poles)
        ]

    def outgoing(i, step):
        return block_copy(i, step, space + 2 * step)

    def incoming(i, step):
        return block_copy(i, step, space - 2 * step)

    def passing(i, at):
        block = both_fields.at[:, pl.ds(at, 2)]
        return [remote(block, block, sib_send.at[i], sib_recv.at[i], pole, sibling)]

    for i in (2, 3, 4, 5, 0, 1):
        @pl.when(has(steps[i]))
        def _():
            for copy in outgoing(i, steps[i]):
                copy.start()

    for copy in passing(6, own):
        copy.start()

    far_copies = [
        remote(param.at[0], param.at[1], far_send.at[0], far_recv.at[0], partner, space),
        remote(stage.at[pl.ds(2, 2), :, pl.ds(0, TOP)], stage_far.at[:, :, pl.ds(0, TOP)],
               far_send.at[1], far_recv.at[1], partner, space),
    ]

    @pl.when(late)
    def _():
        for copy in far_copies:
            copy.start()

    def to_previous(k):
        return remote(fwd.at[pl.ds(2 * k, 2), 1], fwd.at[pl.ds(2 * k, 2), 3],
                      f_send.at[2 * k], f_recv.at[2 * k], pole, space - 1)

    def to_following(k):
        return remote(fwd.at[pl.ds(2 * k, 2), 2], fwd.at[pl.ds(2 * k, 2), 0],
                      f_send.at[2 * k + 1], f_recv.at[2 * k + 1], pole, space + 1)

    def send_forward(k):
        @pl.when(has_previous)
        def _():
            to_previous(k).start()

        @pl.when(has_following)
        def _():
            to_following(k).start()

    def wait_forward(k):
        @pl.when(has_previous)
        def _():
            to_following(k).wait_recv()

        @pl.when(has_following)
        def _():
            to_previous(k).wait_recv()

    def sent_forward(k):
        @pl.when(has_previous)
        def _():
            to_previous(k).wait_send()

        @pl.when(has_following)
        def _():
            to_following(k).wait_send()

    send_forward(0)

    block = (8, 8, NZ)
    row = 8 * lax.broadcasted_iota(jnp.int32, block, 1) + lax.broadcasted_iota(jnp.int32, block, 0)
    col = lax.broadcasted_iota(jnp.int32, block, 2)
    row_first, row_last = row == 0, row == NY - 1
    col_first, col_last = col == 0, col == NZ - 1
    top = row < NY // 2
    col_odd = lax.rem(lax.broadcasted_iota(jnp.int32, (4, 8, NZ), 2), 2) == 1

    def inside(i):
        plane = 4 * chip + i - HALO
        return jnp.logical_and(plane >= 0, plane < 4 * chips)

    def fine_faces(i, odd):
        k = kap[i]
        fx, bx = k + kap[i + 1], k + kap[i - 1]
        py = k + jnp.where(row_last, 0.0, next_row(k))
        qy = jnp.where(row_first, k, previous_row(py))
        pz = k + jnp.where(col_last, 0.0, roll(k, -1, 2))
        qz = jnp.where(col_first, k, roll(pz, 1, 2))
        my, mz = jnp.where(row_last, 0.0, py), jnp.where(col_last, 0.0, pz)
        face_x[i] = fx
        face_y[i] = my
        face_z[i] = mz
        down_z[i] = jnp.where(col_first, 0.0, qz)
        b = (fx + bx) + (py + qy) + (pz + qz)
        base[i] = b
        d = b + own_shift
        g = jnp.where(inside(i), W, 0.0) / d
        diag[i] = d
        gain[i] = g
        z1[i] = g * res[i]
        around = row_pairs(fx if odd else bx), rows_of(qy)[0] + rows_of(py)[1], row_pairs(pz), row_pairs(qz)
        return fx, around, rows_of(my)[1], row_pairs(mz)

    def faces(j):
        i = 2 * j
        _, (bx0, by0, pz0, qz0), fy0, fz0 = fine_faces(i, False)
        fx, (bx1, by1, pz1, qz1), fy1, fz1 = fine_faces(i + 1, True)
        cface_x[j] = pair_sum(fx)
        fy = fy0 + fy1
        cface_y[j] = fy + roll(fy, -1, 2)
        cface_z[j] = roll(fz0 + fz1, -1, 2)
        both = (bx0 + bx1) + (by0 + by1)
        d = both + (qz0 + qz1) + roll(both + (pz0 + pz1), -1, 2)
        cbase[j] = d
        cgain[j] = jnp.where(inside(i), W, 0.0) / (d + 8.0 * own_shift)

    middle = HALO // 2
    other = HALO + 2 * (1 - core)
    for copy in passing(6, other):
        copy.wait_recv()
    for i in (2, 3, 4, 5):
        @pl.when(has(-steps[i]))
        def _():
            for copy in incoming(i, steps[i]):
                copy.wait_recv()
            for copy in share_copy(i, steps[i]):
                copy.start()
    for ring in range(3):
        pair = tuple(enumerate(steps))[2 * ring : 2 * ring + 2]
        for i, step in pair:
            @pl.when(has(-step))
            def _():
                for copy in share_copy(i, step) if ring else incoming(i, step):
                    copy.wait_recv()
                for copy in passing(i, own - 4 * step):
                    copy.start()
        for i, step in pair:
            @pl.when(has(-step))
            def _():
                for copy in passing(i, other - 4 * step):
                    copy.wait_recv()
        take_token(ring)
        send_token(ring + 1)
        if ring == 0:
            rows = (middle - 1, middle, middle + 1, middle + 2)
        else:
            rows = (middle - 2 * ring - 1, middle - 2 * ring, middle + 2 * ring + 1, middle + 2 * ring + 2)
        for j in rows:
            faces(j)
    face_x[0] = kap[0] + kap[1]
    fine_faces(1, True)
    fine_faces(PLANES - 2, False)

    def off(vm, v, vp, fm, fx, fy):
        total = fx * vp + fm * vm
        return total + (fy * next_row(v) + previous_row(fy * v))

    def lane_rolls(fz, v, by):
        return fz * roll(v, -by, 2) + roll(fz * v, by, 2)

    def fine_lanes(i, v):
        if i % 2:
            return lane_rolls(face_z[i], v, 1)
        after, before = lane_sides(v, shifts[...])
        return face_z[i] * after + down_z[i] * before

    def coarse_lanes(j, v):
        return lane_rolls(cface_z[j], v, 2)

    def sweep(ref, lo, hi, faces_xy, lanes, emit):
        px, py = faces_xy
        vm, v, fm = ref[lo - 1], ref[lo], px[lo - 1]
        for i in range(lo, hi):
            vp, fx = ref[i + 1], px[i]
            emit(i, off(vm, v, vp, fm, fx, py[i]) + lanes(i, v), v)
            vm, v, fm = v, vp, fx

    fine_xy, coarse_xy = (face_x, face_y), (cface_x, cface_y)

    def precondition(source, out, lo, hi):
        first, last = (lo - 1) // 2, hi // 2
        held = []

        def down(i, part_off, v):
            held.append(0.2 * source[i] + part_off)
            if i % 2:
                y1[i // 2] = cgain[i // 2] * pair_sum(held[-2] + held[-1])

        def up(j, part_off, v):
            i = 2 * j
            y2 = 1.2 * v + cgain[j] * part_off
            y2 = jnp.where(col_odd, roll(y2, 1, 2), y2)
            y2 = jnp.stack([y2, y2], axis=1).reshape(block)
            z2[i] = z1[i] + y2
            z2[i + 1] = z1[i + 1] + y2

        def smooth(i, part_off, v):
            out[i] = 0.2 * v + z1[i] + gain[i] * part_off

        sweep(z1, 2 * first - 2, 2 * last + 4, fine_xy, fine_lanes, down)
        sweep(y1, first, last + 1, coarse_xy, coarse_lanes, up)
        sweep(z2, lo, hi, fine_xy, fine_lanes, smooth)

    window = HALO - 1 + 2 * core
    sib_window = HALO + 1 - 2 * core

    def exchange(e):
        return [
            remote(mine.at[e, pl.ds(sib_window, 4)], theirs.at[e], xs_send.at[e, a], xs_recv.at[e, a],
                   pole, sibling)
            for a, (mine, theirs) in enumerate(((u0, sib_u), (ut, sib_t)))
        ]

    sub = lax.broadcasted_iota(jnp.int32, (8, NZ), 0)
    lane = lax.broadcasted_iota(jnp.int32, (8, NZ), 1)
    part[0] = jnp.zeros((8, NZ), jnp.float32)

    def solve(e, carry):
        @pl.when(e == 1)
        def _():
            far_copies[0].wait_recv()
            shift = param[1, 0]
            for i in range(1, PLANES - 1):
                d = base[i] + shift
                g = jnp.where(inside(i), W, 0.0) / d
                diag[i] = d
                gain[i] = g
                z1[i] = g * res[i]
            for j in range(1, PLANES // 2 - 1):
                cgain[j] = jnp.where(inside(2 * j), W, 0.0) / (cbase[j] + 8.0 * shift)

        u, t = u0.at[e], ut.at[e]
        precondition(res, u, HALO - 6, HALO + 10)

        def residual(i, part_off, v):
            value = res[i] - (diag[i] * v - part_off)
            rt[i] = value
            z1[i] = gain[i] * value

        sweep(u, HALO - 5, HALO + 9, fine_xy, fine_lanes, residual)
        precondition(rt, t, HALO - 1, HALO + 5)
        for copy in exchange(e):
            copy.start()
        totals = [jnp.zeros((8, NZ), jnp.float32)] * 4

        def products(i, part_off, v):
            image = diag[i] * v - part_off
            un, rn, tn = u[i], res[i], rt[i]
            for k, product in enumerate((un * rn, un * tn, tn * v, v * image)):
                totals[k] = totals[k] + jnp.sum(product, axis=0)

        sweep(t, HALO, HALO + 4, fine_xy, fine_lanes, products)
        tile = part[0]
        for k, total in enumerate(totals):
            tile = jnp.where(sub == 4 * e + k, jnp.sum(total, axis=0, keepdims=True), tile)
        part[0] = tile
        return carry

    lax.fori_loop(0, 2 - half, solve, 0)
    take_token(len(TOKENS) - 1)

    def reduce_start(d, carry):
        remote(part.at[0], part.at[d], ar_send, ar_recv, pole, lax.rem(space + 2 * d, 2 * chips)).start()
        return carry

    lax.fori_loop(1, chips, reduce_start, 0)

    def ahead_row(v):
        return jnp.where(row_last, 0.0, next_row(v))

    def ahead_col(v):
        return jnp.where(col_last, 0.0, roll(v, -1, 2))

    def slot_terms(e, who, fields, at):
        slot = 2 * e + (core if who == 0 else 1 - core)
        for n in (1, 2):
            f = fwd[slot, n]
            f_next, f_last = f - fwd[slot, n + 1], f - fwd[slot, n - 1]
            f_row, f_col = f - ahead_row(f), f - ahead_col(f)
            for k, ref in enumerate(fields):
                x = ref[at + n]
                total = (x - ref[at + n + 1]) * f_next + (x - ref[at + n - 1]) * f_last
                product = x * f
                ahead = (x - ahead_row(x)) * f_row
                total = total + ahead + jnp.where(row_first, product, previous_row(ahead))
                ahead = (x - ahead_col(x)) * f_col
                parts[e, who, k, n - 1] = total + ahead + jnp.where(col_first, product, roll(ahead, 1, 2))

    for copy in exchange(0):
        copy.wait_recv()
    wait_forward(0)
    slot_terms(0, 0, (u0.at[0], ut.at[0]), window)
    slot_terms(0, 1, (sib_u.at[0], sib_t.at[0]), 0)

    @pl.when(early)
    def _():
        far_copies[1].wait_recv()
        for slot in range(2):
            for n in range(2):
                fwd[2 + slot, 1 + n] = natural(stage_far, (slot, n))
        send_forward(1)
        for copy in exchange(1):
            copy.wait_recv()
        wait_forward(1)
        slot_terms(1, 0, (u0.at[1], ut.at[1]), window)
        slot_terms(1, 1, (sib_u.at[1], sib_t.at[1]), 0)

    def everyone(sem):
        return pltpu.make_async_copy(part.at[pl.ds(1, chips - 1)], part.at[pl.ds(1, chips - 1)], sem)

    everyone(ar_recv).wait()
    total = jnp.sum(jnp.sum(part[...], axis=0), axis=1, keepdims=True)
    factors = []
    for e in range(2):
        g0, d0, e1, m0 = (total[4 * e + k : 4 * e + k + 1] for k in range(4))
        weight = param[e, 1][0:1, 0:1]
        c0 = g0 - d0
        eta = d0 / c0
        a0 = 1.0 + eta
        t = d0 - e1
        k = c0 - t
        g1 = e1 - 2.0 * eta * t + eta * eta * k
        b = g1 / g0
        s11 = m0 - 2.0 * eta * (t - m0) + eta * eta * (k - t + m0)
        c1 = s11 + 2.0 * b * (t - eta * k) + b * b * c0
        a1 = g1 / c1
        factors += [weight * (a0 + a1 * (b - eta)), weight * (a1 * a0)]
    tile = jnp.broadcast_to(factors[0], (8, NZ))
    for k in range(1, 4):
        tile = jnp.where(lane == k, factors[k], tile)
    sums[...] = tile
    scalars = remote(sums, swap, sw_send, sw_recv, pole, sibling)
    scalars.start()
    scalars.wait_recv()

    def weighted(e, n):
        factor = [ref[0:1, 2 * e + k : 2 * e + k + 1] for ref in (sums, swap) for k in range(2)]
        own_part = factor[0] * parts[e, 0, 0, n] + factor[1] * parts[e, 0, 1, n]
        return own_part + (factor[2] * parts[e, 1, 0, n] + factor[3] * parts[e, 1, 1, n])

    @pl.when(late)
    def _():
        for n in range(2):
            put_natural(term, (n,), -0.5 * weighted(0, n))

    @pl.when(early)
    def _():
        for n in range(2):
            put_natural(term, (n,), -0.5 * (weighted(0, n) + jnp.where(top, weighted(1, n), 0.0)))

    def rows_for(q):
        return pl.ds(pl.multiple_of(8 * q, 8), 8)

    def spread(d, upper):
        q = lax.rem(yy + d, half_poles)
        k = 0 if upper else 1
        return remote(term.at[:, rows_for(q if upper else q + half_poles), :], pieces.at[k, d],
                      rs_send.at[k, d], rs_recv.at[k, d], half * half_poles + q, space)

    @pl.when(early)
    def _():
        for d in range(1, half_poles):
            spread(d, True).start()

    for d in range(1, half_poles):
        spread(d, False).start()

    for ref, fields, at, slot in ((sums, (u0.at[0], ut.at[0]), window, core), (swap, (sib_u.at[0], sib_t.at[0]), 0, 1 - core)):
        for n in range(2):
            value = ref[0:1, 0:1] * fields[0][at + 1 + n] + ref[0:1, 1:2] * fields[1][at + 1 + n]
            put_natural(adjoint_ref, (slot, n), value)

    share = remote(gfar, gnear, far_send.at[2], far_recv.at[2], partner, space)

    def collect(k, q):
        total = term[:, rows_for(q), :]
        for d in range(1, half_poles):
            spread(d, k == 0).wait_recv()
            total = total + pieces[k, d]
        return total

    @pl.when(early)
    def _():
        gradient_ref[...] = collect(0, yy)
        gfar[...] = collect(1, yy + half_poles)
        share.start()

    @pl.when(late)
    def _():
        total = collect(1, yy + half_poles)
        share.wait_recv()
        gradient_ref[...] = total + gnear[...]

    for i, step in enumerate(steps):
        @pl.when(has(step))
        def _():
            for copy in outgoing(i, step):
                copy.wait_send()

        @pl.when(has(-step))
        def _():
            for copy in passing(i, own - 4 * step):
                copy.wait_send()
            if abs(step) >= 2:
                for copy in share_copy(i, step):
                    copy.wait_send()
    for copy in passing(6, own):
        copy.wait_send()
    sent_forward(0)
    for copy in exchange(0):
        copy.wait_send()
    everyone(ar_send).wait()
    scalars.wait_send()
    for d in range(1, half_poles):
        spread(d, False).wait_send()

    @pl.when(early)
    def _():
        sent_forward(1)
        for copy in exchange(1):
            copy.wait_send()
        for d in range(1, half_poles):
            spread(d, True).wait_send()
        share.wait_send()

    @pl.when(late)
    def _():
        for copy in far_copies:
            copy.wait_send()


def solution(mesh):
    chips, poles = mesh.shape["space"] // 2, mesh.shape["pole"]
    f32 = jnp.float32

    def per_device(conductivity, misfit, forward_states, pole_shifts, pole_weights, pole_order):
        hbm, vmem = pl.BlockSpec(memory_space=pltpu.HBM), pl.BlockSpec(memory_space=pltpu.VMEM)
        fine = pltpu.VMEM((PLANES, 8, 8, NZ), f32)
        coarse = pltpu.VMEM((PLANES // 2, 4, 8, NZ), f32)
        pair = pltpu.VMEM((2, PLANES, 8, 8, NZ), f32)
        windows = pltpu.VMEM((2, 4, 8, 8, NZ), f32)
        slots = pltpu.VMEM((4, 4, 8, 8, NZ), f32)
        tile = pltpu.VMEM((8, NZ), f32)
        piece = (2, NY // poles, NZ)
        dma = pltpu.SemaphoreType.DMA
        return pl.pallas_call(
            functools.partial(kernel, chips, poles),
            out_shape=(
                pltpu.VMEM(forward_states.shape, f32),
                pltpu.VMEM(piece, f32),
            ),
            in_specs=[hbm] * 6,
            out_specs=(vmem, vmem),
            scratch_shapes=[
                pltpu.SMEM(pole_shifts.shape, f32), pltpu.SMEM(pole_weights.shape, f32),
                pltpu.SMEM(pole_order.shape, jnp.int32),
            ] + [pltpu.VMEM((2, PLANES, 8, 8, NZ), f32)] + [fine] * 10 + [coarse] * 6 + [
                pair, pair, windows, windows, slots, pltpu.VMEM((2, 2, 2, 2, 8, 8, NZ), f32),
                pltpu.VMEM((4, 2, NY, NZ), f32), pltpu.VMEM((2, 2, NY, NZ), f32),
                pltpu.VMEM((2, NY, NZ), f32), pltpu.VMEM((2, 2, 8, NZ), f32),
                pltpu.VMEM((chips, 8, NZ), f32), tile, tile,
                pltpu.VMEM((2, poles // 2, *piece), f32), pltpu.VMEM(piece, f32), pltpu.VMEM(piece, f32),
                pltpu.VMEM((3 * NZ, 2 * NZ), jnp.bfloat16),
                dma((6,)), dma((6,)), dma((6,)), dma((7,)), dma((7,)), dma((4,)), dma((4,)),
                dma, dma, dma, dma, dma((2, 2)), dma((2, 2)),
                dma((2, poles // 2)), dma((2, poles // 2)), dma((3,)), dma((3,)),
                dma((4, poles // 2)), dma((4, poles // 2)), pltpu.SemaphoreType.REGULAR((len(TOKENS), 2)),
            ],
            compiler_params=pltpu.CompilerParams(
                collective_id=0, has_side_effects=True, vmem_limit_bytes=62 << 20
            ),
            name="adjoint_gradient",
        )(pole_shifts, pole_weights, pole_order, conductivity, misfit, forward_states)

    in_specs = (
        P("space", None, None), P("space", None, None), P("pole", "space", None, None),
        P(), P(), P("pole"),
    )
    out_specs = (P("pole", "space", None, None), P("space", "pole", None))
    return jax.shard_map(per_device, mesh=mesh, in_specs=in_specs, out_specs=out_specs, check_vma=False)
```

```python
import functools

import jax
import jax.numpy as jnp
from jax import lax
from jax.experimental import pallas as pl
from jax.experimental.pallas import tpu as pltpu
from jax.sharding import PartitionSpec as P

MESH = pl.DeviceIdType.MESH
W = 0.8
NY, NZ = 64, 128
HALO = 12
PLANES = 4 + 2 * HALO
TOKENS = (3, 6, 12, 24)
TOP = NY // 2 + 8


def roll(value, shift, axis):
    return pltpu.roll(value, shift % value.shape[axis], axis)


def next_row(value):
    return jnp.concatenate([value[1:], roll(value[:1], -1, 1)], axis=0)


def previous_row(value):
    return jnp.concatenate([roll(value[-1:], 1, 1), value[:-1]], axis=0)


def rows_of(value):
    pairs = value.reshape(value.shape[0] // 2, 2, *value.shape[1:])
    return pairs[:, 0], pairs[:, 1]


def row_pairs(value):
    even, odd = rows_of(value)
    return even + odd


def pair_sum(value):
    value = row_pairs(value)
    return value + roll(value, -1, 2)


def lane_sides(value, shifts):
    rows = value.reshape(-1, NZ)
    high = rows.astype(jnp.bfloat16)
    rest = rows - high.astype(jnp.float32)
    mid = rest.astype(jnp.bfloat16)
    low = (rest - mid.astype(jnp.float32)).astype(jnp.bfloat16)
    out = jnp.dot(jnp.concatenate([high, mid, low], axis=1), shifts, preferred_element_type=jnp.float32)
    return out[:, :NZ].reshape(value.shape), out[:, NZ:].reshape(value.shape)


def natural(ref, index):
    return jnp.stack([ref[(*index, pl.ds(v, 8, stride=8), slice(None))] for v in range(8)])


def put_natural(ref, index, value):
    for v in range(8):
        ref[(*index, pl.ds(v, 8, stride=8), slice(None))] = value[v]


def kernel(
    chips, poles,
    shift_ref, weight_ref, order_ref, kappa_ref, misfit_ref, forward_ref,
    adjoint_ref, gradient_ref,
    shift_mem, weight_mem, order_mem,
    both_fields, face_x, face_y, face_z, down_z, base, diag, gain, z1, z2, rt,
    cface_x, cface_y, cface_z, cbase, cgain, y1, u0, ut,
    sib_u, sib_t, fwd, parts, stage, stage_far, term, param, part, sums, swap, pieces, gfar, gnear, shifts,
    loc, near_send, near_recv, sib_send, sib_recv, f_send, f_recv, ar_send, ar_recv, sw_send, sw_recv,
    xs_send, xs_recv, rs_send, rs_recv, far_send, far_recv, y_send, y_recv, token,
):
    half_poles = poles // 2
    kap, res = both_fields.at[0], both_fields.at[1]
    pole = lax.axis_index("pole")
    space = lax.axis_index("space")
    half, yy = pole // half_poles, lax.rem(pole, half_poles)
    early, late = half == 0, half == 1
    partner = lax.rem(pole + half_poles, poles)
    core = lax.rem(space, 2)
    chip = space // 2
    sibling = space + 1 - 2 * core
    has_previous, has_following = space > 0, space < 2 * chips - 1
    steps = (1, -1, 2, -2, 3, -3)

    def has(step):
        return jnp.logical_and(chip + step >= 0, chip + step < chips)

    own = HALO + 2 * core
    own_copies = [
        pltpu.make_async_copy(kappa_ref, stage.at[0], loc.at[0]),
        pltpu.make_async_copy(misfit_ref, stage.at[1], loc.at[1]),
        pltpu.make_async_copy(forward_ref, stage.at[pl.ds(2, 2)], loc.at[2]),
        pltpu.make_async_copy(shift_ref, shift_mem, loc.at[3]),
        pltpu.make_async_copy(weight_ref, weight_mem, loc.at[4]),
        pltpu.make_async_copy(order_ref, order_mem, loc.at[5]),
    ]
    for copy in own_copies:
        copy.start()

    barrier = pltpu.get_barrier_semaphore()

    def greet(p, s):
        pl.semaphore_signal(barrier, inc=1, device_id=(p, s), device_id_type=MESH)

    across = space + 2 * core - 1
    has_across = jnp.logical_and(across >= 0, across < 2 * chips)
    expected = half_poles + has_across.astype(jnp.int32) + late.astype(jnp.int32)
    for step in steps:
        expected = expected + has(step).astype(jnp.int32)

        @pl.when(has(step))
        def _():
            greet(pole, space + 2 * step)

    greet(pole, sibling)

    @pl.when(has_across)
    def _():
        greet(pole, across)

    for d in range(1, half_poles):
        greet(half * half_poles + lax.rem(yy + d, half_poles), space)

    @pl.when(early)
    def _():
        greet(partner, space)

    for copy in own_copies:
        copy.wait()
    for n in range(2):
        kap[own + n] = 0.5 * natural(stage, (0, n))
        res[own + n] = natural(stage, (1, n))
        for slot in range(2):
            fwd[slot, 1 + n] = natural(stage, (2 + slot, n))
    pole_here = order_mem[core]
    own_shift = shift_mem[pole_here]
    param[0, 0] = jnp.full((8, NZ), own_shift, jnp.float32)
    param[0, 1] = jnp.full((8, NZ), weight_mem[pole_here], jnp.float32)

    pl.semaphore_wait(barrier, expected)

    def send_token(k):
        for a, step in enumerate((TOKENS[k], -TOKENS[k])):
            @pl.when(has(step))
            def _():
                pl.semaphore_signal(token.at[k, a], inc=1, device_id=(pole, space + 2 * step), device_id_type=MESH)

    def take_token(k):
        for a, step in enumerate((TOKENS[k], -TOKENS[k])):
            @pl.when(has(-step))
            def _():
                pl.semaphore_wait(token.at[k, a], 1)

    send_token(0)

    def remote(src, dst, send, recv, p, s):
        return pltpu.make_async_remote_copy(
            src_ref=src, dst_ref=dst, send_sem=send, recv_sem=recv,
            device_id=(p, s), device_id_type=MESH,
        )

    part_rows = 8 // half_poles
    my_part = pl.ds(part_rows * yy, part_rows)

    def block_copy(i, step, target):
        share = (my_part,) if abs(step) >= 2 else ()
        return [
            remote(both_fields.at[(slice(None), pl.ds(own, 2), *share)],
                   both_fields.at[(slice(None), pl.ds(own - 4 * step, 2), *share)],
                   near_send.at[i], near_recv.at[i], pole, target)
        ]

    def share_copy(i, step):
        block = both_fields.at[:, pl.ds(own - 4 * step, 2), my_part]
        return [
            remote(block, block, y_send.at[i - 2, d], y_recv.at[i - 2, d],
                   half * half_poles + lax.rem(yy + d, half_poles), space)
            for d in range(1, half_poles)
        ]

    def outgoing(i, step):
        return block_copy(i, step, space + 2 * step)

    def incoming(i, step):
        return block_copy(i, step, space - 2 * step)

    def passing(i, at):
        block = both_fields.at[:, pl.ds(at, 2)]
        return [remote(block, block, sib_send.at[i], sib_recv.at[i], pole, sibling)]

    far_copies = [
        remote(param.at[0], param.at[1], far_send.at[0], far_recv.at[0], partner, space),
        remote(stage.at[pl.ds(2, 2), :, pl.ds(0, TOP)], stage_far.at[:, :, pl.ds(0, TOP)],
               far_send.at[1], far_recv.at[1], partner, space),
    ]

    @pl.when(late)
    def _():
        far_copies[0].start()

    for i in (2, 3, 4, 5, 0, 1):
        @pl.when(has(steps[i]))
        def _():
            for copy in outgoing(i, steps[i]):
                copy.start()

    for copy in passing(6, own):
        copy.start()

    @pl.when(late)
    def _():
        far_copies[1].start()

    def to_previous(k):
        return remote(fwd.at[pl.ds(2 * k, 2), 1], fwd.at[pl.ds(2 * k, 2), 3],
                      f_send.at[2 * k], f_recv.at[2 * k], pole, space - 1)

    def to_following(k):
        return remote(fwd.at[pl.ds(2 * k, 2), 2], fwd.at[pl.ds(2 * k, 2), 0],
                      f_send.at[2 * k + 1], f_recv.at[2 * k + 1], pole, space + 1)

    def send_forward(k):
        @pl.when(has_previous)
        def _():
            to_previous(k).start()

        @pl.when(has_following)
        def _():
            to_following(k).start()

    def wait_forward(k):
        @pl.when(has_previous)
        def _():
            to_following(k).wait_recv()

        @pl.when(has_following)
        def _():
            to_previous(k).wait_recv()

    def sent_forward(k):
        @pl.when(has_previous)
        def _():
            to_previous(k).wait_send()

        @pl.when(has_following)
        def _():
            to_following(k).wait_send()

    send_forward(0)

    for step in steps:
        @pl.when(jnp.logical_not(has(step)))
        def _():
            zeros = jnp.zeros((4, 8, 8, NZ), jnp.float32)
            kap[pl.ds(HALO + 4 * step, 4)] = zeros
            res[pl.ds(HALO + 4 * step, 4)] = zeros

    @pl.when(jnp.logical_not(has_previous))
    def _():
        fwd[:, 0] = jnp.zeros((4, 8, 8, NZ), jnp.float32)

    @pl.when(jnp.logical_not(has_following))
    def _():
        fwd[:, 3] = jnp.zeros((4, 8, 8, NZ), jnp.float32)

    stage_far[:, :, TOP:] = jnp.zeros((2, 2, NY - TOP, NZ), jnp.float32)
    lane_in = lax.broadcasted_iota(jnp.int32, (NZ, NZ), 0)
    lane_out = lax.broadcasted_iota(jnp.int32, (NZ, NZ), 1)
    for a, by in enumerate((1, -1)):
        matrix = jnp.where(lane_in == lane_out + by, 1.0, 0.0).astype(jnp.bfloat16)
        for k in range(3):
            shifts[NZ * k : NZ * (k + 1), NZ * a : NZ * (a + 1)] = matrix

    block = (8, 8, NZ)
    row = 8 * lax.broadcasted_iota(jnp.int32, block, 1) + lax.broadcasted_iota(jnp.int32, block, 0)
    col = lax.broadcasted_iota(jnp.int32, block, 2)
    row_first, row_last = row == 0, row == NY - 1
    col_first, col_last = col == 0, col == NZ - 1
    top = row < NY // 2
    col_odd = lax.rem(lax.broadcasted_iota(jnp.int32, (4, 8, NZ), 2), 2) == 1

    def inside(i):
        plane = 4 * chip + i - HALO
        return jnp.logical_and(plane >= 0, plane < 4 * chips)

    def fine_faces(i, odd):
        k = kap[i]
        fx, bx = k + kap[i + 1], k + kap[i - 1]
        py = k + jnp.where(row_last, 0.0, next_row(k))
        qy = jnp.where(row_first, k, previous_row(py))
        if odd:
            after, before = roll(k, -1, 2), roll(k, 1, 2)
        else:
            after, before = lane_sides(k, shifts[...])
        pz = k + jnp.where(col_last, 0.0, after)
        qz = k + jnp.where(col_first, 0.0, before)
        my, mz = jnp.where(row_last, 0.0, py), jnp.where(col_last, 0.0, pz)
        face_x[i] = fx
        face_y[i] = my
        face_z[i] = mz
        down_z[i] = jnp.where(col_first, 0.0, qz)
        b = (fx + bx) + (py + qy) + (pz + qz)
        base[i] = b
        d = b + own_shift
        g = jnp.where(inside(i), W, 0.0) / d
        diag[i] = d
        gain[i] = g
        z1[i] = g * res[i]
        around = row_pairs(fx if odd else bx), rows_of(qy)[0] + rows_of(py)[1], row_pairs(pz), row_pairs(qz)
        return fx, around, rows_of(my)[1], row_pairs(mz)

    def faces(j):
        i = 2 * j
        _, (bx0, by0, pz0, qz0), fy0, fz0 = fine_faces(i, False)
        fx, (bx1, by1, pz1, qz1), fy1, fz1 = fine_faces(i + 1, True)
        cface_x[j] = pair_sum(fx)
        fy = fy0 + fy1
        cface_y[j] = fy + roll(fy, -1, 2)
        cface_z[j] = roll(fz0 + fz1, -1, 2)
        both = (bx0 + bx1) + (by0 + by1)
        d = both + (qz0 + qz1) + roll(both + (pz0 + pz1), -1, 2)
        cbase[j] = d
        cgain[j] = jnp.where(inside(i), W, 0.0) / (d + 8.0 * own_shift)

    middle = HALO // 2
    other = HALO + 2 * (1 - core)
    for copy in passing(6, other):
        copy.wait_recv()
    for i in (2, 3, 4, 5):
        @pl.when(has(-steps[i]))
        def _():
            for copy in incoming(i, steps[i]):
                copy.wait_recv()
            for copy in share_copy(i, steps[i]):
                copy.start()
    for ring in range(3):
        pair = tuple(enumerate(steps))[2 * ring : 2 * ring + 2]
        for i, step in pair:
            @pl.when(has(-step))
            def _():
                for copy in share_copy(i, step) if ring else incoming(i, step):
                    copy.wait_recv()
                for copy in passing(i, own - 4 * step):
                    copy.start()
        for i, step in pair:
            @pl.when(has(-step))
            def _():
                for copy in passing(i, other - 4 * step):
                    copy.wait_recv()
        take_token(ring)
        send_token(ring + 1)
        if ring == 0:
            rows = (middle - 1, middle, middle + 1, middle + 2)
        else:
            rows = (middle - 2 * ring - 1, middle - 2 * ring, middle + 2 * ring + 1, middle + 2 * ring + 2)
        for j in rows:
            faces(j)
    face_x[0] = kap[0] + kap[1]
    fine_faces(1, True)
    fine_faces(PLANES - 2, False)

    def off(vm, v, vp, fm, fx, fy):
        total = fx * vp + fm * vm
        return total + (fy * next_row(v) + previous_row(fy * v))

    def lane_rolls(fz, v, by):
        return fz * roll(v, -by, 2) + roll(fz * v, by, 2)

    def fine_lanes(i, v):
        if i % 2:
            return lane_rolls(face_z[i], v, 1)
        after, before = lane_sides(v, shifts[...])
        return face_z[i] * after + down_z[i] * before

    def coarse_lanes(j, v):
        return lane_rolls(cface_z[j], v, 2)

    def sweep(ref, lo, hi, faces_xy, lanes, emit):
        px, py = faces_xy
        vm, v, fm = ref[lo - 1], ref[lo], px[lo - 1]
        for i in range(lo, hi):
            vp, fx = ref[i + 1], px[i]
            emit(i, off(vm, v, vp, fm, fx, py[i]) + lanes(i, v), v)
            vm, v, fm = v, vp, fx

    fine_xy, coarse_xy = (face_x, face_y), (cface_x, cface_y)

    def precondition(source, out, lo, hi):
        first, last = (lo - 1) // 2, hi // 2
        held = []

        def down(i, part_off, v):
            held.append(0.2 * source[i] + part_off)
            if i % 2:
                y1[i // 2] = cgain[i // 2] * pair_sum(held[-2] + held[-1])

        def up(j, part_off, v):
            i = 2 * j
            y2 = 1.2 * v + cgain[j] * part_off
            y2 = jnp.where(col_odd, roll(y2, 1, 2), y2)
            y2 = jnp.stack([y2, y2], axis=1).reshape(block)
            z2[i] = z1[i] + y2
            z2[i + 1] = z1[i + 1] + y2

        def smooth(i, part_off, v):
            out[i] = 0.2 * v + z1[i] + gain[i] * part_off

        sweep(z1, 2 * first - 2, 2 * last + 4, fine_xy, fine_lanes, down)
        sweep(y1, first, last + 1, coarse_xy, coarse_lanes, up)
        sweep(z2, lo, hi, fine_xy, fine_lanes, smooth)

    window = HALO - 1 + 2 * core
    sib_window = HALO + 1 - 2 * core

    def exchange(e):
        return [
            remote(mine.at[e, pl.ds(sib_window, 4)], theirs.at[e], xs_send.at[e, a], xs_recv.at[e, a],
                   pole, sibling)
            for a, (mine, theirs) in enumerate(((u0, sib_u), (ut, sib_t)))
        ]

    sub = lax.broadcasted_iota(jnp.int32, (8, NZ), 0)
    lane = lax.broadcasted_iota(jnp.int32, (8, NZ), 1)
    part[0] = jnp.zeros((8, NZ), jnp.float32)

    def solve(e, carry):
        @pl.when(e == 1)
        def _():
            far_copies[0].wait_recv()
            shift = param[1, 0]
            for i in range(1, PLANES - 1):
                d = base[i] + shift
                g = jnp.where(inside(i), W, 0.0) / d
                diag[i] = d
                gain[i] = g
                z1[i] = g * res[i]
            for j in range(1, PLANES // 2 - 1):
                cgain[j] = jnp.where(inside(2 * j), W, 0.0) / (cbase[j] + 8.0 * shift)

        u, t = u0.at[e], ut.at[e]
        precondition(res, u, HALO - 6, HALO + 10)

        def residual(i, part_off, v):
            value = res[i] - (diag[i] * v - part_off)
            rt[i] = value
            z1[i] = gain[i] * value

        sweep(u, HALO - 5, HALO + 9, fine_xy, fine_lanes, residual)
        precondition(rt, t, HALO - 1, HALO + 5)
        for copy in exchange(e):
            copy.start()
        totals = [jnp.zeros((8, NZ), jnp.float32)] * 4

        def products(i, part_off, v):
            image = diag[i] * v - part_off
            un, rn, tn = u[i], res[i], rt[i]
            for k, product in enumerate((un * rn, un * tn, tn * v, v * image)):
                totals[k] = totals[k] + jnp.sum(product, axis=0)

        sweep(t, HALO, HALO + 4, fine_xy, fine_lanes, products)
        tile = part[0]
        for k, total in enumerate(totals):
            tile = jnp.where(sub == 4 * e + k, jnp.sum(total, axis=0, keepdims=True), tile)
        part[0] = tile
        return carry

    lax.fori_loop(0, 2 - half, solve, 0)
    take_token(len(TOKENS) - 1)

    def reduce_start(d, carry):
        remote(part.at[0], part.at[d], ar_send, ar_recv, pole, lax.rem(space + 2 * d, 2 * chips)).start()
        return carry

    lax.fori_loop(1, chips, reduce_start, 0)

    def ahead_row(v):
        return jnp.where(row_last, 0.0, next_row(v))

    def ahead_col(v):
        return jnp.where(col_last, 0.0, roll(v, -1, 2))

    def slot_terms(e, who, fields, at):
        slot = 2 * e + (core if who == 0 else 1 - core)
        for n in (1, 2):
            f = fwd[slot, n]
            f_next, f_last = f - fwd[slot, n + 1], f - fwd[slot, n - 1]
            f_row, f_col = f - ahead_row(f), f - ahead_col(f)
            for k, ref in enumerate(fields):
                x = ref[at + n]
                total = (x - ref[at + n + 1]) * f_next + (x - ref[at + n - 1]) * f_last
                product = x * f
                ahead = (x - ahead_row(x)) * f_row
                total = total + ahead + jnp.where(row_first, product, previous_row(ahead))
                ahead = (x - ahead_col(x)) * f_col
                parts[e, who, k, n - 1] = total + ahead + jnp.where(col_first, product, roll(ahead, 1, 2))

    for copy in exchange(0):
        copy.wait_recv()
    wait_forward(0)
    slot_terms(0, 0, (u0.at[0], ut.at[0]), window)
    slot_terms(0, 1, (sib_u.at[0], sib_t.at[0]), 0)

    @pl.when(early)
    def _():
        far_copies[1].wait_recv()
        for slot in range(2):
            for n in range(2):
                fwd[2 + slot, 1 + n] = natural(stage_far, (slot, n))
        send_forward(1)
        for copy in exchange(1):
            copy.wait_recv()
        wait_forward(1)
        slot_terms(1, 0, (u0.at[1], ut.at[1]), window)
        slot_terms(1, 1, (sib_u.at[1], sib_t.at[1]), 0)

    def everyone(sem):
        return pltpu.make_async_copy(part.at[pl.ds(1, chips - 1)], part.at[pl.ds(1, chips - 1)], sem)

    everyone(ar_recv).wait()
    total = jnp.sum(jnp.sum(part[...], axis=0), axis=1, keepdims=True)
    factors = []
    for e in range(2):
        g0, d0, e1, m0 = (total[4 * e + k : 4 * e + k + 1] for k in range(4))
        weight = param[e, 1][0:1, 0:1]
        c0 = g0 - d0
        eta = d0 / c0
        a0 = 1.0 + eta
        t = d0 - e1
        k = c0 - t
        g1 = e1 - 2.0 * eta * t + eta * eta * k
        b = g1 / g0
        s11 = m0 - 2.0 * eta * (t - m0) + eta * eta * (k - t + m0)
        c1 = s11 + 2.0 * b * (t - eta * k) + b * b * c0
        a1 = g1 / c1
        factors += [weight * (a0 + a1 * (b - eta)), weight * (a1 * a0)]
    tile = jnp.broadcast_to(factors[0], (8, NZ))
    for k in range(1, 4):
        tile = jnp.where(lane == k, factors[k], tile)
    sums[...] = tile
    scalars = remote(sums, swap, sw_send, sw_recv, pole, sibling)
    scalars.start()
    scalars.wait_recv()

    def weighted(e, n):
        factor = [ref[0:1, 2 * e + k : 2 * e + k + 1] for ref in (sums, swap) for k in range(2)]
        own_part = factor[0] * parts[e, 0, 0, n] + factor[1] * parts[e, 0, 1, n]
        return own_part + (factor[2] * parts[e, 1, 0, n] + factor[3] * parts[e, 1, 1, n])

    @pl.when(late)
    def _():
        for n in range(2):
            put_natural(term, (n,), -0.5 * weighted(0, n))

    @pl.when(early)
    def _():
        for n in range(2):
            put_natural(term, (n,), -0.5 * (weighted(0, n) + jnp.where(top, weighted(1, n), 0.0)))

    def rows_for(q):
        return pl.ds(pl.multiple_of(8 * q, 8), 8)

    def spread(d, upper):
        q = lax.rem(yy + d, half_poles)
        k = 0 if upper else 1
        return remote(term.at[:, rows_for(q if upper else q + half_poles), :], pieces.at[k, d],
                      rs_send.at[k, d], rs_recv.at[k, d], half * half_poles + q, space)

    @pl.when(early)
    def _():
        for d in range(1, half_poles):
            spread(d, True).start()

    for d in range(1, half_poles):
        spread(d, False).start()

    for ref, fields, at, slot in ((sums, (u0.at[0], ut.at[0]), window, core), (swap, (sib_u.at[0], sib_t.at[0]), 0, 1 - core)):
        for n in range(2):
            value = ref[0:1, 0:1] * fields[0][at + 1 + n] + ref[0:1, 1:2] * fields[1][at + 1 + n]
            put_natural(adjoint_ref, (slot, n), value)

    share = remote(gfar, gnear, far_send.at[2], far_recv.at[2], partner, space)

    def collect(k, q):
        total = term[:, rows_for(q), :]
        for d in range(1, half_poles):
            spread(d, k == 0).wait_recv()
            total = total + pieces[k, d]
        return total

    @pl.when(early)
    def _():
        gradient_ref[...] = collect(0, yy)
        gfar[...] = collect(1, yy + half_poles)
        share.start()

    @pl.when(late)
    def _():
        total = collect(1, yy + half_poles)
        share.wait_recv()
        gradient_ref[...] = total + gnear[...]

    for i, step in enumerate(steps):
        @pl.when(has(step))
        def _():
            for copy in outgoing(i, step):
                copy.wait_send()

        @pl.when(has(-step))
        def _():
            for copy in passing(i, own - 4 * step):
                copy.wait_send()
            if abs(step) >= 2:
                for copy in share_copy(i, step):
                    copy.wait_send()
    for copy in passing(6, own):
        copy.wait_send()
    sent_forward(0)
    for copy in exchange(0):
        copy.wait_send()
    everyone(ar_send).wait()
    scalars.wait_send()
    for d in range(1, half_poles):
        spread(d, False).wait_send()

    @pl.when(early)
    def _():
        sent_forward(1)
        for copy in exchange(1):
            copy.wait_send()
        for d in range(1, half_poles):
            spread(d, True).wait_send()
        share.wait_send()

    @pl.when(late)
    def _():
        for copy in far_copies:
            copy.wait_send()


def solution(mesh):
    chips, poles = mesh.shape["space"] // 2, mesh.shape["pole"]
    f32 = jnp.float32

    def per_device(conductivity, misfit, forward_states, pole_shifts, pole_weights, pole_order):
        hbm, vmem = pl.BlockSpec(memory_space=pltpu.HBM), pl.BlockSpec(memory_space=pltpu.VMEM)
        fine = pltpu.VMEM((PLANES, 8, 8, NZ), f32)
        coarse = pltpu.VMEM((PLANES // 2, 4, 8, NZ), f32)
        pair = pltpu.VMEM((2, PLANES, 8, 8, NZ), f32)
        windows = pltpu.VMEM((2, 4, 8, 8, NZ), f32)
        slots = pltpu.VMEM((4, 4, 8, 8, NZ), f32)
        tile = pltpu.VMEM((8, NZ), f32)
        piece = (2, NY // poles, NZ)
        dma = pltpu.SemaphoreType.DMA
        return pl.pallas_call(
            functools.partial(kernel, chips, poles),
            out_shape=(
                pltpu.VMEM(forward_states.shape, f32),
                pltpu.VMEM(piece, f32),
            ),
            in_specs=[hbm] * 6,
            out_specs=(vmem, vmem),
            scratch_shapes=[
                pltpu.SMEM(pole_shifts.shape, f32), pltpu.SMEM(pole_weights.shape, f32),
                pltpu.SMEM(pole_order.shape, jnp.int32),
            ] + [pltpu.VMEM((2, PLANES, 8, 8, NZ), f32)] + [fine] * 10 + [coarse] * 6 + [
                pair, pair, windows, windows, slots, pltpu.VMEM((2, 2, 2, 2, 8, 8, NZ), f32),
                pltpu.VMEM((4, 2, NY, NZ), f32), pltpu.VMEM((2, 2, NY, NZ), f32),
                pltpu.VMEM((2, NY, NZ), f32), pltpu.VMEM((2, 2, 8, NZ), f32),
                pltpu.VMEM((chips, 8, NZ), f32), tile, tile,
                pltpu.VMEM((2, poles // 2, *piece), f32), pltpu.VMEM(piece, f32), pltpu.VMEM(piece, f32),
                pltpu.VMEM((3 * NZ, 2 * NZ), jnp.bfloat16),
                dma((6,)), dma((6,)), dma((6,)), dma((7,)), dma((7,)), dma((4,)), dma((4,)),
                dma, dma, dma, dma, dma((2, 2)), dma((2, 2)),
                dma((2, poles // 2)), dma((2, poles // 2)), dma((3,)), dma((3,)),
                dma((4, poles // 2)), dma((4, poles // 2)), pltpu.SemaphoreType.REGULAR((len(TOKENS), 2)),
            ],
            compiler_params=pltpu.CompilerParams(
                collective_id=0, has_side_effects=True, vmem_limit_bytes=62 << 20
            ),
            name="adjoint_gradient",
        )(pole_shifts, pole_weights, pole_order, conductivity, misfit, forward_states)

    in_specs = (
        P("space", None, None), P("space", None, None), P("pole", "space", None, None),
        P(), P(), P("pole"),
    )
    out_specs = (P("pole", "space", None, None), P("space", "pole", None))
    return jax.shard_map(per_device, mesh=mesh, in_specs=in_specs, out_specs=out_specs, check_vma=False)
```

```python
import functools

import jax
import jax.numpy as jnp
from jax import lax
from jax.experimental import pallas as pl
from jax.experimental.pallas import tpu as pltpu
from jax.sharding import PartitionSpec as P

MESH = pl.DeviceIdType.MESH
W = 0.8
NY, NZ = 64, 128
HALO = 12
PLANES = 4 + 2 * HALO
TOKENS = (3, 6, 12, 24)
TOP = NY // 2 + 8


def roll(value, shift, axis):
    return pltpu.roll(value, shift % value.shape[axis], axis)


def next_row(value):
    return jnp.concatenate([value[1:], roll(value[:1], -1, 1)], axis=0)


def previous_row(value):
    return jnp.concatenate([roll(value[-1:], 1, 1), value[:-1]], axis=0)


def rows_of(value):
    pairs = value.reshape(value.shape[0] // 2, 2, *value.shape[1:])
    return pairs[:, 0], pairs[:, 1]


def row_pairs(value):
    even, odd = rows_of(value)
    return even + odd


def pair_sum(value):
    value = row_pairs(value)
    return value + roll(value, -1, 2)


def lane_sides(value, shifts):
    rows = value.reshape(-1, NZ)
    high = rows.astype(jnp.bfloat16)
    rest = rows - high.astype(jnp.float32)
    mid = rest.astype(jnp.bfloat16)
    low = (rest - mid.astype(jnp.float32)).astype(jnp.bfloat16)
    out = jnp.dot(jnp.concatenate([high, mid, low], axis=1), shifts, preferred_element_type=jnp.float32)
    return out[:, :NZ].reshape(value.shape), out[:, NZ:].reshape(value.shape)


def natural(ref, index):
    return jnp.stack([ref[(*index, pl.ds(v, 8, stride=8), slice(None))] for v in range(8)])


def put_natural(ref, index, value):
    for v in range(8):
        ref[(*index, pl.ds(v, 8, stride=8), slice(None))] = value[v]


def kernel(
    chips, poles,
    shift_ref, weight_ref, order_ref, kappa_ref, misfit_ref, forward_ref,
    adjoint_ref, gradient_ref,
    shift_mem, weight_mem, order_mem,
    both_fields, face_x, face_y, face_z, down_z, base, z2, rt,
    cface_x, cface_y, cface_z, cbase, y1, cgain, diag, gain, z1, u0, ut,
    sib_u, sib_t, fwd, parts, stage, stage_far, term, param, part, sums, swap, pieces, gfar, gnear, shifts,
    loc, near_send, near_recv, sib_send, sib_recv, f_send, f_recv, ar_send, ar_recv, sw_send, sw_recv,
    xs_send, xs_recv, rs_send, rs_recv, far_send, far_recv, y_send, y_recv, token,
):
    half_poles = poles // 2
    kap, res = both_fields.at[0], both_fields.at[1]
    pole = lax.axis_index("pole")
    space = lax.axis_index("space")
    half, yy = pole // half_poles, lax.rem(pole, half_poles)
    early, late = half == 0, half == 1
    partner = lax.rem(pole + half_poles, poles)
    core = lax.rem(space, 2)
    chip = space // 2
    sibling = space + 1 - 2 * core
    has_previous, has_following = space > 0, space < 2 * chips - 1
    steps = (1, -1, 2, -2, 3, -3)

    def has(step):
        return jnp.logical_and(chip + step >= 0, chip + step < chips)

    own = HALO + 2 * core
    own_copies = [
        pltpu.make_async_copy(kappa_ref, stage.at[0], loc.at[0]),
        pltpu.make_async_copy(misfit_ref, stage.at[1], loc.at[1]),
        pltpu.make_async_copy(forward_ref, stage.at[pl.ds(2, 2)], loc.at[2]),
        pltpu.make_async_copy(shift_ref, shift_mem, loc.at[3]),
        pltpu.make_async_copy(weight_ref, weight_mem, loc.at[4]),
        pltpu.make_async_copy(order_ref, order_mem, loc.at[5]),
    ]
    for copy in own_copies:
        copy.start()

    barrier = pltpu.get_barrier_semaphore()

    def greet(p, s):
        pl.semaphore_signal(barrier, inc=1, device_id=(p, s), device_id_type=MESH)

    across = space + 2 * core - 1
    has_across = jnp.logical_and(across >= 0, across < 2 * chips)
    expected = half_poles + has_across.astype(jnp.int32) + late.astype(jnp.int32)
    for step in steps:
        expected = expected + has(step).astype(jnp.int32)

        @pl.when(has(step))
        def _():
            greet(pole, space + 2 * step)

    greet(pole, sibling)

    @pl.when(has_across)
    def _():
        greet(pole, across)

    for d in range(1, half_poles):
        greet(half * half_poles + lax.rem(yy + d, half_poles), space)

    @pl.when(early)
    def _():
        greet(partner, space)

    for copy in own_copies:
        copy.wait()
    for n in range(2):
        kap[own + n] = 0.5 * natural(stage, (0, n))
        res[own + n] = natural(stage, (1, n))
        for slot in range(2):
            fwd[slot, 1 + n] = natural(stage, (2 + slot, n))
    pole_here = order_mem[core]
    own_shift = shift_mem[pole_here]
    param[0, 0] = jnp.full((8, NZ), own_shift, jnp.float32)
    param[0, 1] = jnp.full((8, NZ), weight_mem[pole_here], jnp.float32)

    pl.semaphore_wait(barrier, expected)

    def send_token(k):
        for a, step in enumerate((TOKENS[k], -TOKENS[k])):
            @pl.when(has(step))
            def _():
                pl.semaphore_signal(token.at[k, a], inc=1, device_id=(pole, space + 2 * step), device_id_type=MESH)

    def take_token(k):
        for a, step in enumerate((TOKENS[k], -TOKENS[k])):
            @pl.when(has(-step))
            def _():
                pl.semaphore_wait(token.at[k, a], 1)

    send_token(0)

    def remote(src, dst, send, recv, p, s):
        return pltpu.make_async_remote_copy(
            src_ref=src, dst_ref=dst, send_sem=send, recv_sem=recv,
            device_id=(p, s), device_id_type=MESH,
        )

    part_rows = 8 // half_poles
    my_part = pl.ds(part_rows * yy, part_rows)

    def block_copy(i, step, target):
        share = (my_part,) if abs(step) >= 2 else ()
        return [
            remote(both_fields.at[(slice(None), pl.ds(own, 2), *share)],
                   both_fields.at[(slice(None), pl.ds(own - 4 * step, 2), *share)],
                   near_send.at[i], near_recv.at[i], pole, target)
        ]

    def share_copy(i, step):
        block = both_fields.at[:, pl.ds(own - 4 * step, 2), my_part]
        return [
            remote(block, block, y_send.at[i - 2, d], y_recv.at[i - 2, d],
                   half * half_poles + lax.rem(yy + d, half_poles), space)
            for d in (half_poles // 2, *(d for d in range(1, half_poles) if d != half_poles // 2))
        ]

    def outgoing(i, step):
        return block_copy(i, step, space + 2 * step)

    def incoming(i, step):
        return block_copy(i, step, space - 2 * step)

    def passing(i, at):
        block = both_fields.at[:, pl.ds(at, 2)]
        return [remote(block, block, sib_send.at[i], sib_recv.at[i], pole, sibling)]

    far_copies = [
        remote(param.at[0], param.at[1], far_send.at[0], far_recv.at[0], partner, space),
        remote(stage.at[pl.ds(2, 2), :, pl.ds(0, TOP)], stage_far.at[:, :, pl.ds(0, TOP)],
               far_send.at[1], far_recv.at[1], partner, space),
    ]

    @pl.when(late)
    def _():
        far_copies[0].start()

    for i in (2, 3, 4, 5, 0, 1):
        @pl.when(has(steps[i]))
        def _():
            for copy in outgoing(i, steps[i]):
                copy.start()

    for copy in passing(6, own):
        copy.start()

    @pl.when(late)
    def _():
        far_copies[1].start()

    def to_previous(k):
        return remote(fwd.at[pl.ds(2 * k, 2), 1], fwd.at[pl.ds(2 * k, 2), 3],
                      f_send.at[2 * k], f_recv.at[2 * k], pole, space - 1)

    def to_following(k):
        return remote(fwd.at[pl.ds(2 * k, 2), 2], fwd.at[pl.ds(2 * k, 2), 0],
                      f_send.at[2 * k + 1], f_recv.at[2 * k + 1], pole, space + 1)

    def send_forward(k):
        @pl.when(has_previous)
        def _():
            to_previous(k).start()

        @pl.when(has_following)
        def _():
            to_following(k).start()

    def wait_forward(k):
        @pl.when(has_previous)
        def _():
            to_following(k).wait_recv()

        @pl.when(has_following)
        def _():
            to_previous(k).wait_recv()

    def sent_forward(k):
        @pl.when(has_previous)
        def _():
            to_previous(k).wait_send()

        @pl.when(has_following)
        def _():
            to_following(k).wait_send()

    send_forward(0)

    for step in steps:
        @pl.when(jnp.logical_not(has(step)))
        def _():
            zeros = jnp.zeros((4, 8, 8, NZ), jnp.float32)
            kap[pl.ds(HALO + 4 * step, 4)] = zeros
            res[pl.ds(HALO + 4 * step, 4)] = zeros

    @pl.when(jnp.logical_not(has_previous))
    def _():
        fwd[:, 0] = jnp.zeros((4, 8, 8, NZ), jnp.float32)

    @pl.when(jnp.logical_not(has_following))
    def _():
        fwd[:, 3] = jnp.zeros((4, 8, 8, NZ), jnp.float32)

    stage_far[:, :, TOP:] = jnp.zeros((2, 2, NY - TOP, NZ), jnp.float32)
    lane_in = lax.broadcasted_iota(jnp.int32, (NZ, NZ), 0)
    lane_out = lax.broadcasted_iota(jnp.int32, (NZ, NZ), 1)
    for a, by in enumerate((1, -1)):
        matrix = jnp.where(lane_in == lane_out + by, 1.0, 0.0).astype(jnp.bfloat16)
        for k in range(3):
            shifts[NZ * k : NZ * (k + 1), NZ * a : NZ * (a + 1)] = matrix

    block = (8, 8, NZ)
    row = 8 * lax.broadcasted_iota(jnp.int32, block, 1) + lax.broadcasted_iota(jnp.int32, block, 0)
    col = lax.broadcasted_iota(jnp.int32, block, 2)
    row_first, row_last = row == 0, row == NY - 1
    col_first, col_last = col == 0, col == NZ - 1
    top = row < NY // 2
    col_odd = lax.rem(lax.broadcasted_iota(jnp.int32, (4, 8, NZ), 2), 2) == 1

    def inside(i):
        plane = 4 * chip + i - HALO
        return jnp.logical_and(plane >= 0, plane < 4 * chips)

    def fine_faces(i, odd):
        k = kap[i]
        fx, bx = k + kap[i + 1], k + kap[i - 1]
        py = k + jnp.where(row_last, 0.0, next_row(k))
        qy = jnp.where(row_first, k, previous_row(py))
        if odd:
            after, before = roll(k, -1, 2), roll(k, 1, 2)
        else:
            after, before = lane_sides(k, shifts[...])
        pz = k + jnp.where(col_last, 0.0, after)
        qz = k + jnp.where(col_first, 0.0, before)
        my, mz = jnp.where(row_last, 0.0, py), jnp.where(col_last, 0.0, pz)
        face_x[i] = fx
        face_y[i] = my
        face_z[i] = mz
        down_z[i] = jnp.where(col_first, 0.0, qz)
        b = (fx + bx) + (py + qy) + (pz + qz)
        base[i] = b
        d = b + own_shift
        g = jnp.where(inside(i), W, 0.0) / d
        diag[0, i] = d
        gain[0, i] = g
        z1[0, i] = g * res[i]
        around = row_pairs(fx if odd else bx), rows_of(qy)[0] + rows_of(py)[1], row_pairs(pz), row_pairs(qz)
        return fx, around, rows_of(my)[1], row_pairs(mz)

    def faces(j):
        i = 2 * j
        _, (bx0, by0, pz0, qz0), fy0, fz0 = fine_faces(i, False)
        fx, (bx1, by1, pz1, qz1), fy1, fz1 = fine_faces(i + 1, True)
        cface_x[j] = pair_sum(fx)
        fy = fy0 + fy1
        cface_y[j] = fy + roll(fy, -1, 2)
        cface_z[j] = roll(fz0 + fz1, -1, 2)
        both = (bx0 + bx1) + (by0 + by1)
        d = both + (qz0 + qz1) + roll(both + (pz0 + pz1), -1, 2)
        cbase[j] = d
        cgain[0, j] = jnp.where(inside(i), W, 0.0) / (d + 8.0 * own_shift)

    def far_gain(i, shift):
        d = base[i] + shift
        g = jnp.where(inside(i), W, 0.0) / d
        diag[1, i] = d
        gain[1, i] = g
        z1[1, i] = g * res[i]

    def far_gains(rows):
        shift = param[1, 0]
        for j in rows:
            far_gain(2 * j, shift)
            far_gain(2 * j + 1, shift)
            cgain[1, j] = jnp.where(inside(2 * j), W, 0.0) / (cbase[j] + 8.0 * shift)

    middle = HALO // 2
    other = HALO + 2 * (1 - core)
    for copy in passing(6, other):
        copy.wait_recv()
    for i in (2, 3, 4, 5):
        @pl.when(has(-steps[i]))
        def _():
            for copy in incoming(i, steps[i]):
                copy.wait_recv()
            for copy in share_copy(i, steps[i]):
                copy.start()
    for ring in range(3):
        pair = tuple(enumerate(steps))[2 * ring : 2 * ring + 2]
        for i, step in pair:
            @pl.when(has(-step))
            def _():
                for copy in share_copy(i, step) if ring else incoming(i, step):
                    copy.wait_recv()
                for copy in passing(i, own - 4 * step):
                    copy.start()
        for i, step in pair:
            @pl.when(has(-step))
            def _():
                for copy in passing(i, other - 4 * step):
                    copy.wait_recv()
        take_token(ring)
        send_token(ring + 1)
        if ring == 0:
            rows = (middle - 1, middle, middle + 1, middle + 2)
        else:
            rows = (middle - 2 * ring - 1, middle - 2 * ring, middle + 2 * ring + 1, middle + 2 * ring + 2)
        for j in rows:
            faces(j)
        if ring == 1:
            @pl.when(early)
            def _():
                far_copies[0].wait_recv()
                far_gains(range(middle - 3, middle + 5))
    face_x[0] = kap[0] + kap[1]
    fine_faces(1, True)
    fine_faces(PLANES - 2, False)

    @pl.when(early)
    def _():
        far_gains((*range(1, middle - 3), *range(middle + 5, PLANES // 2 - 1)))
        far_gain(1, param[1, 0])
        far_gain(PLANES - 2, param[1, 0])

    def off(vm, v, vp, fm, fx, fy):
        total = fx * vp + fm * vm
        return total + (fy * next_row(v) + previous_row(fy * v))

    def lane_rolls(fz, v, by):
        return fz * roll(v, -by, 2) + roll(fz * v, by, 2)

    def fine_lanes(i, v):
        if i % 2:
            return lane_rolls(face_z[i], v, 1)
        after, before = lane_sides(v, shifts[...])
        return face_z[i] * after + down_z[i] * before

    def coarse_lanes(j, v):
        return lane_rolls(cface_z[j], v, 2)

    def sweep(ref, lo, hi, faces_xy, lanes, emit):
        px, py = faces_xy
        vm, v, fm = ref[lo - 1], ref[lo], px[lo - 1]
        for i in range(lo, hi):
            vp, fx = ref[i + 1], px[i]
            emit(i, off(vm, v, vp, fm, fx, py[i]) + lanes(i, v), v)
            vm, v, fm = v, vp, fx

    fine_xy, coarse_xy = (face_x, face_y), (cface_x, cface_y)

    def precondition(e, source, out, lo, hi):
        start = z1.at[e]
        first, last = (lo - 1) // 2, hi // 2
        held = []

        def down(i, part_off, v):
            held.append(0.2 * source[i] + part_off)
            if i % 2:
                y1[i // 2] = cgain[e, i // 2] * pair_sum(held[-2] + held[-1])

        def up(j, part_off, v):
            i = 2 * j
            y2 = 1.2 * v + cgain[e, j] * part_off
            y2 = jnp.where(col_odd, roll(y2, 1, 2), y2)
            y2 = jnp.stack([y2, y2], axis=1).reshape(block)
            z2[i] = start[i] + y2
            z2[i + 1] = start[i + 1] + y2

        def smooth(i, part_off, v):
            out[i] = 0.2 * v + start[i] + gain[e, i] * part_off

        sweep(start, 2 * first - 2, 2 * last + 4, fine_xy, fine_lanes, down)
        sweep(y1, first, last + 1, coarse_xy, coarse_lanes, up)
        sweep(z2, lo, hi, fine_xy, fine_lanes, smooth)

    window = HALO - 1 + 2 * core
    sib_window = HALO + 1 - 2 * core

    def exchange(e):
        return [
            remote(mine.at[e, pl.ds(sib_window, 4)], theirs.at[e], xs_send.at[e, a], xs_recv.at[e, a],
                   pole, sibling)
            for a, (mine, theirs) in enumerate(((u0, sib_u), (ut, sib_t)))
        ]

    sub = lax.broadcasted_iota(jnp.int32, (8, NZ), 0)
    lane = lax.broadcasted_iota(jnp.int32, (8, NZ), 1)
    part[0] = jnp.zeros((8, NZ), jnp.float32)

    def solve(e, carry):
        u, t = u0.at[e], ut.at[e]
        precondition(e, res, u, HALO - 6, HALO + 10)

        def residual(i, part_off, v):
            value = res[i] - (diag[e, i] * v - part_off)
            rt[i] = value
            z1[e, i] = gain[e, i] * value

        sweep(u, HALO - 5, HALO + 9, fine_xy, fine_lanes, residual)
        precondition(e, rt, t, HALO - 1, HALO + 5)
        for copy in exchange(e):
            copy.start()
        totals = [jnp.zeros((8, NZ), jnp.float32)] * 4

        def products(i, part_off, v):
            image = diag[e, i] * v - part_off
            un, rn, tn = u[i], res[i], rt[i]
            for k, product in enumerate((un * rn, un * tn, tn * v, v * image)):
                totals[k] = totals[k] + jnp.sum(product, axis=0)

        sweep(t, HALO, HALO + 4, fine_xy, fine_lanes, products)
        tile = part[0]
        for k, total in enumerate(totals):
            tile = jnp.where(sub == 4 * e + k, jnp.sum(total, axis=0, keepdims=True), tile)
        part[0] = tile
        return carry

    lax.fori_loop(0, 2 - half, solve, 0)
    take_token(len(TOKENS) - 1)

    def reduce_start(d, carry):
        remote(part.at[0], part.at[d], ar_send, ar_recv, pole, lax.rem(space + 2 * d, 2 * chips)).start()
        return carry

    lax.fori_loop(1, chips, reduce_start, 0)

    def ahead_row(v):
        return jnp.where(row_last, 0.0, next_row(v))

    def ahead_col(v):
        return jnp.where(col_last, 0.0, roll(v, -1, 2))

    def slot_terms(e, who, fields, at):
        slot = 2 * e + (core if who == 0 else 1 - core)
        for n in (1, 2):
            f = fwd[slot, n]
            f_next, f_last = f - fwd[slot, n + 1], f - fwd[slot, n - 1]
            f_row, f_col = f - ahead_row(f), f - ahead_col(f)
            for k, ref in enumerate(fields):
                x = ref[at + n]
                total = (x - ref[at + n + 1]) * f_next + (x - ref[at + n - 1]) * f_last
                product = x * f
                ahead = (x - ahead_row(x)) * f_row
                total = total + ahead + jnp.where(row_first, product, previous_row(ahead))
                ahead = (x - ahead_col(x)) * f_col
                parts[e, who, k, n - 1] = total + ahead + jnp.where(col_first, product, roll(ahead, 1, 2))

    for copy in exchange(0):
        copy.wait_recv()
    wait_forward(0)
    slot_terms(0, 0, (u0.at[0], ut.at[0]), window)
    slot_terms(0, 1, (sib_u.at[0], sib_t.at[0]), 0)

    @pl.when(early)
    def _():
        far_copies[1].wait_recv()
        for slot in range(2):
            for n in range(2):
                fwd[2 + slot, 1 + n] = natural(stage_far, (slot, n))
        send_forward(1)
        for copy in exchange(1):
            copy.wait_recv()
        wait_forward(1)
        slot_terms(1, 0, (u0.at[1], ut.at[1]), window)
        slot_terms(1, 1, (sib_u.at[1], sib_t.at[1]), 0)

    def everyone(sem):
        return pltpu.make_async_copy(part.at[pl.ds(1, chips - 1)], part.at[pl.ds(1, chips - 1)], sem)

    everyone(ar_recv).wait()
    total = jnp.sum(jnp.sum(part[...], axis=0), axis=1, keepdims=True)
    factors = []
    for e in range(2):
        g0, d0, e1, m0 = (total[4 * e + k : 4 * e + k + 1] for k in range(4))
        weight = param[e, 1][0:1, 0:1]
        c0 = g0 - d0
        eta = d0 / c0
        a0 = 1.0 + eta
        t = d0 - e1
        k = c0 - t
        g1 = e1 - 2.0 * eta * t + eta * eta * k
        b = g1 / g0
        s11 = m0 - 2.0 * eta * (t - m0) + eta * eta * (k - t + m0)
        c1 = s11 + 2.0 * b * (t - eta * k) + b * b * c0
        a1 = g1 / c1
        factors += [weight * (a0 + a1 * (b - eta)), weight * (a1 * a0)]
    tile = jnp.broadcast_to(factors[0], (8, NZ))
    for k in range(1, 4):
        tile = jnp.where(lane == k, factors[k], tile)
    sums[...] = tile
    scalars = remote(sums, swap, sw_send, sw_recv, pole, sibling)
    scalars.start()
    scalars.wait_recv()

    def weighted(e, n):
        factor = [ref[0:1, 2 * e + k : 2 * e + k + 1] for ref in (sums, swap) for k in range(2)]
        own_part = factor[0] * parts[e, 0, 0, n] + factor[1] * parts[e, 0, 1, n]
        return own_part + (factor[2] * parts[e, 1, 0, n] + factor[3] * parts[e, 1, 1, n])

    @pl.when(late)
    def _():
        for n in range(2):
            put_natural(term, (n,), -0.5 * weighted(0, n))

    @pl.when(early)
    def _():
        for n in range(2):
            put_natural(term, (n,), -0.5 * (weighted(0, n) + jnp.where(top, weighted(1, n), 0.0)))

    def rows_for(q):
        return pl.ds(pl.multiple_of(8 * q, 8), 8)

    def spread(d, upper):
        q = lax.rem(yy + d, half_poles)
        k = 0 if upper else 1
        return remote(term.at[:, rows_for(q if upper else q + half_poles), :], pieces.at[k, d],
                      rs_send.at[k, d], rs_recv.at[k, d], half * half_poles + q, space)

    @pl.when(early)
    def _():
        for d in range(1, half_poles):
            spread(d, True).start()

    for d in range(1, half_poles):
        spread(d, False).start()

    for ref, fields, at, slot in ((sums, (u0.at[0], ut.at[0]), window, core), (swap, (sib_u.at[0], sib_t.at[0]), 0, 1 - core)):
        for n in range(2):
            value = ref[0:1, 0:1] * fields[0][at + 1 + n] + ref[0:1, 1:2] * fields[1][at + 1 + n]
            put_natural(adjoint_ref, (slot, n), value)

    share = remote(gfar, gnear, far_send.at[2], far_recv.at[2], partner, space)

    def collect(k, q):
        total = term[:, rows_for(q), :]
        for d in range(1, half_poles):
            spread(d, k == 0).wait_recv()
            total = total + pieces[k, d]
        return total

    @pl.when(early)
    def _():
        gradient_ref[...] = collect(0, yy)
        gfar[...] = collect(1, yy + half_poles)
        share.start()

    @pl.when(late)
    def _():
        total = collect(1, yy + half_poles)
        share.wait_recv()
        gradient_ref[...] = total + gnear[...]

    for i, step in enumerate(steps):
        @pl.when(has(step))
        def _():
            for copy in outgoing(i, step):
                copy.wait_send()

        @pl.when(has(-step))
        def _():
            for copy in passing(i, own - 4 * step):
                copy.wait_send()
            if abs(step) >= 2:
                for copy in share_copy(i, step):
                    copy.wait_send()
    for copy in passing(6, own):
        copy.wait_send()
    sent_forward(0)
    for copy in exchange(0):
        copy.wait_send()
    everyone(ar_send).wait()
    scalars.wait_send()
    for d in range(1, half_poles):
        spread(d, False).wait_send()

    @pl.when(early)
    def _():
        sent_forward(1)
        for copy in exchange(1):
            copy.wait_send()
        for d in range(1, half_poles):
            spread(d, True).wait_send()
        share.wait_send()

    @pl.when(late)
    def _():
        for copy in far_copies:
            copy.wait_send()


def solution(mesh):
    chips, poles = mesh.shape["space"] // 2, mesh.shape["pole"]
    f32 = jnp.float32

    def per_device(conductivity, misfit, forward_states, pole_shifts, pole_weights, pole_order):
        hbm, vmem = pl.BlockSpec(memory_space=pltpu.HBM), pl.BlockSpec(memory_space=pltpu.VMEM)
        fine = pltpu.VMEM((PLANES, 8, 8, NZ), f32)
        coarse = pltpu.VMEM((PLANES // 2, 4, 8, NZ), f32)
        pair = pltpu.VMEM((2, PLANES, 8, 8, NZ), f32)
        windows = pltpu.VMEM((2, 4, 8, 8, NZ), f32)
        slots = pltpu.VMEM((4, 4, 8, 8, NZ), f32)
        tile = pltpu.VMEM((8, NZ), f32)
        piece = (2, NY // poles, NZ)
        dma = pltpu.SemaphoreType.DMA
        return pl.pallas_call(
            functools.partial(kernel, chips, poles),
            out_shape=(
                pltpu.VMEM(forward_states.shape, f32),
                pltpu.VMEM(piece, f32),
            ),
            in_specs=[hbm] * 6,
            out_specs=(vmem, vmem),
            scratch_shapes=[
                pltpu.SMEM(pole_shifts.shape, f32), pltpu.SMEM(pole_weights.shape, f32),
                pltpu.SMEM(pole_order.shape, jnp.int32),
            ] + [pltpu.VMEM((2, PLANES, 8, 8, NZ), f32)] + [fine] * 7 + [coarse] * 5 + [
                pltpu.VMEM((2, PLANES // 2, 4, 8, NZ), f32), pair, pair, pair, pair, pair, windows, windows, slots, pltpu.VMEM((2, 2, 2, 2, 8, 8, NZ), f32),
                pltpu.VMEM((4, 2, NY, NZ), f32), pltpu.VMEM((2, 2, NY, NZ), f32),
                pltpu.VMEM((2, NY, NZ), f32), pltpu.VMEM((2, 2, 8, NZ), f32),
                pltpu.VMEM((chips, 8, NZ), f32), tile, tile,
                pltpu.VMEM((2, poles // 2, *piece), f32), pltpu.VMEM(piece, f32), pltpu.VMEM(piece, f32),
                pltpu.VMEM((3 * NZ, 2 * NZ), jnp.bfloat16),
                dma((6,)), dma((6,)), dma((6,)), dma((7,)), dma((7,)), dma((4,)), dma((4,)),
                dma, dma, dma, dma, dma((2, 2)), dma((2, 2)),
                dma((2, poles // 2)), dma((2, poles // 2)), dma((3,)), dma((3,)),
                dma((4, poles // 2)), dma((4, poles // 2)), pltpu.SemaphoreType.REGULAR((len(TOKENS), 2)),
            ],
            compiler_params=pltpu.CompilerParams(
                collective_id=0, has_side_effects=True, vmem_limit_bytes=62 << 20
            ),
            name="adjoint_gradient",
        )(pole_shifts, pole_weights, pole_order, conductivity, misfit, forward_states)

    in_specs = (
        P("space", None, None), P("space", None, None), P("pole", "space", None, None),
        P(), P(), P("pole"),
    )
    out_specs = (P("pole", "space", None, None), P("space", "pole", None))
    return jax.shard_map(per_device, mesh=mesh, in_specs=in_specs, out_specs=out_specs, check_vma=False)
```
